128 devices in a mesh: row: 8 (over x_hi, z), col: 16 (over x_lo, y, core).
Axes of the slice: x: 4 (x_hi: 2, x_lo: 2; x = x_hi * 2 + x_lo), y: 4, z: 4, core: 2. Of those that a mesh axis runs over, the one named last changes fastest.
Arguments:
- left: float32 [2, 8192, 2560], P(None, 'row', 'col'), may hold values from -6 to 6
- right: float32 [2, 2560, 8192], P(None, 'row', 'col'), may hold values from -0.078125 to 0.078125
- prefix_owner: int32 [64], replicated, may hold values from 0 to 63, each once
- qubit_order: int32 [7], replicated, may hold values from 0 to 6, each once
Outputs:
- relaid: float32 [2, 8192, 8192], P(None, ('row', 'col'))
The draws below stay inside these ranges and needn't reach their ends.
Inputs may be any that keep to these rules, and one draw needn't show every extreme that they name: `prefix_owner`: each prefix has exactly one owner, each owner one prefix. `qubit_order`: each open qubit appears once.
All inputs are finite; a program needn't handle non-finite values.
Results may differ from the reference program's by a relative error of at most 0.00007.
Values sent between devices are 32-bit elements; how exact they have to be, the bound alone decides.
A program may use at most 192 MiB of HBM per device.

```python
import jax
import jax.numpy as jnp
from jax import lax

N = 8192
LOW_BITS = 7
PREFIXES = 64
K = 2560
M = 8192


def shard_levels(own_key, shape, cuts, low, high):
    level, own = 1.0, jax.random.fold_in(own_key, 6)
    for dim, parts in cuts:
        heights = jnp.exp(jax.random.uniform(jax.random.fold_in(own, dim), (parts,), jnp.float32, low / len(cuts), high / len(cuts)))
        level = level * jnp.repeat(heights, shape[dim] // parts).reshape([-1 if axis == dim else 1 for axis in range(len(shape))])
    return level


def centred(stream_key, shape, scale, most, shards=(), held_as=jnp.bfloat16):
    factor_of = shard_levels(stream_key, shape, shards, -0.22, 0.18) if shards else 1.0
    entries = jax.random.normal(stream_key, shape, jnp.float32) * scale * factor_of
    return jnp.minimum(jnp.maximum(entries, -most), most).astype(held_as)


def setup_inputs(seed: int = 0) -> dict:
    key_of = jax.random.split(jax.random.key(seed), 5)
    left = centred(key_of[0], (2, M, K), 1.0, 6.0, ((1, 8), (2, 16)), jnp.float32)
    right = centred(key_of[1], (2, K, N), (2 * K) ** -0.5, 0.078125, ((1, 8), (2, 16)), jnp.float32)
    prefix_owner = jax.random.permutation(key_of[2], PREFIXES).astype(jnp.int32)
    qubit_order = jax.random.permutation(key_of[3], LOW_BITS).astype(jnp.int32)
    return dict(left=left, right=right, prefix_owner=prefix_owner, qubit_order=qubit_order)


def source_rows(prefix_owner, qubit_order, total, low_bits, prefixes):
    span = 2 ** low_bits
    index = jnp.arange(total, dtype=jnp.int32)
    owner = index // span
    offset = index % span
    labels = jnp.arange(prefixes, dtype=jnp.int32)
    match = (prefix_owner[None, :] == labels[:, None]).astype(jnp.int32)
    inverse = jnp.sum(match * labels[None, :], axis=1).astype(jnp.int32)
    prefix = jnp.take(inverse, owner, axis=0)
    bits = jnp.bitwise_and(jnp.right_shift(offset[:, None], qubit_order[None, :]), 1)
    powers = jnp.left_shift(jnp.ones((low_bits,), jnp.int32), jnp.arange(low_bits, dtype=jnp.int32))
    inner = jnp.sum(bits * powers[None, :], axis=1).astype(jnp.int32)
    return (prefix * span + inner).astype(jnp.int32)


def reference(left, right, prefix_owner, qubit_order):
    highest = lax.Precision.HIGHEST
    real_part = jnp.dot(left[0], right[0], preferred_element_type=jnp.float32, precision=highest) - jnp.dot(left[1], right[1], preferred_element_type=jnp.float32, precision=highest)
    imag_part = jnp.dot(left[0], right[1], preferred_element_type=jnp.float32, precision=highest) + jnp.dot(left[1], right[0], preferred_element_type=jnp.float32, precision=highest)
    source = source_rows(prefix_owner, qubit_order, M, LOW_BITS, PREFIXES)
    return jnp.stack([jnp.take(real_part, source, axis=0), jnp.take(imag_part, source, axis=0)], axis=0)
```

```python
import jax
import jax.numpy as jnp
import numpy as np
from jax import lax
from jax.sharding import Mesh
from jax.sharding import PartitionSpec as P

LOW_BITS = 7
PREFIXES = 64

ROW = ("xh", "z")
CHIPS = ("xl", "y")
CORE = "core"
COL = ("xl", "y", "core")


def inverse_owner(prefix_owner, prefixes):
    labels = jnp.arange(prefixes, dtype=jnp.int32)
    match = (prefix_owner[None, :] == labels[:, None]).astype(jnp.int32)
    return jnp.sum(match * labels[None, :], axis=1)


def inner_order(qubit_order, low_bits):
    span = 2**low_bits
    offset = jnp.arange(span, dtype=jnp.int32)
    bits = jnp.bitwise_and(jnp.right_shift(offset[:, None], qubit_order[None, :]), 1)
    powers = jnp.left_shift(jnp.ones((low_bits,), jnp.int32), jnp.arange(low_bits, dtype=jnp.int32))
    return jnp.sum(bits * powers[None, :], axis=1)


def permute_left(left, prefix_owner, qubit_order, row_count):
    _, rows, kcols = left.shape
    span = 2**LOW_BITS
    local = rows // span
    sub = span // row_count
    x = left.reshape(2, local, row_count, sub, kcols)
    x = lax.all_to_all(x, ROW, split_axis=2, concat_axis=2, tiled=True)
    x = x.reshape(2, local * row_count, sub, kcols)
    inv = inverse_owner(prefix_owner, PREFIXES)
    pick = (inv % local) * row_count + inv // local
    y = jnp.take(x, pick, axis=1)
    y = y.reshape(2, row_count, local, sub, kcols)
    y = lax.all_to_all(y, ROW, split_axis=1, concat_axis=1, tiled=True)
    y = y.reshape(2, row_count * local * sub, kcols)
    s = inner_order(qubit_order, LOW_BITS)
    o_local = jnp.arange(local, dtype=jnp.int32)
    idx = (s[None, :] // sub) * (local * sub) + o_local[:, None] * sub + s[None, :] % sub
    return jnp.take(y, idx.reshape(-1), axis=1)


def body(left, right, prefix_owner, qubit_order):
    row_count = lax.axis_size(ROW)
    col_count = lax.axis_size(COL)
    rows = left.shape[1]
    cols = right.shape[2]
    lp = permute_left(left, prefix_owner, qubit_order, row_count)
    lp = lax.all_gather(lp, CHIPS, axis=2, tiled=True)
    lp = lax.all_gather(lp, CORE, axis=2, tiled=True)
    depth = right.shape[1]
    halves = lax.axis_size(CORE)
    rr = right.reshape(2, halves, depth // halves, cols)
    rr = lax.all_gather(rr, ROW, axis=2, tiled=True)
    rr = rr.reshape(2, -1, cols)
    high = lax.Precision.HIGH
    dot = lambda a, b: jnp.dot(a, b, preferred_element_type=jnp.float32, precision=high)
    t1 = dot(lp[0], rr[0])
    t2 = dot(lp[1], rr[1])
    t3 = dot(lp[0] + lp[1], rr[0] + rr[1])
    tile = jnp.stack([t1 - t2, t3 - t1 - t2], axis=0)
    tile = tile.reshape(2, col_count, rows // col_count, cols)
    out = lax.all_to_all(tile, COL, split_axis=1, concat_axis=3, tiled=True)
    return out.reshape(2, rows // col_count, col_count * cols)


def solution(mesh):
    devices = np.asarray(mesh.devices)
    nr, nc = devices.shape
    fine = Mesh(devices.reshape(2, nr // 2, 2, nc // 4, 2), ("xh", "z", "xl", "y", "core"))
    in_specs = (P(None, ROW, COL), P(None, ROW, COL), P(), P())
    out_specs = P(None, ROW + COL, None)
    return jax.shard_map(body, mesh=fine, in_specs=in_specs, out_specs=out_specs, check_vma=False)
```

```python
import functools

import jax
import jax.numpy as jnp
import numpy as np
from jax import lax
from jax.experimental import pallas as pl
from jax.experimental.pallas import tpu as pltpu
from jax.sharding import Mesh
from jax.sharding import PartitionSpec as P

LOW_BITS = 7
PREFIXES = 64

ROW = ("xh", "z")
CHIPS = ("xl", "y")
CORE = "core"
COL = ("xl", "y", "core")


def inverse_owner(prefix_owner, prefixes):
    labels = jnp.arange(prefixes, dtype=jnp.int32)
    match = (prefix_owner[None, :] == labels[:, None]).astype(jnp.int32)
    return jnp.sum(match * labels[None, :], axis=1)


def inner_order(qubit_order, low_bits):
    span = 2**low_bits
    offset = jnp.arange(span, dtype=jnp.int32)
    bits = jnp.bitwise_and(jnp.right_shift(offset[:, None], qubit_order[None, :]), 1)
    powers = jnp.left_shift(jnp.ones((low_bits,), jnp.int32), jnp.arange(low_bits, dtype=jnp.int32))
    return jnp.sum(bits * powers[None, :], axis=1)


def permute_left(left, prefix_owner, qubit_order, row_count):
    _, rows, kcols = left.shape
    span = 2**LOW_BITS
    local = rows // span
    sub = span // row_count
    x = left.reshape(2, local, row_count, sub, kcols)
    x = lax.all_to_all(x, ROW, split_axis=2, concat_axis=2, tiled=True)
    x = x.reshape(2, local * row_count, sub, kcols)
    inv = inverse_owner(prefix_owner, PREFIXES)
    pick = (inv % local) * row_count + inv // local
    y = jnp.take(x, pick, axis=1)
    y = y.reshape(2, row_count, local, sub, kcols)
    y = lax.all_to_all(y, ROW, split_axis=1, concat_axis=1, tiled=True)
    y = y.reshape(2, row_count * local * sub, kcols)
    s = inner_order(qubit_order, LOW_BITS)
    o_local = jnp.arange(local, dtype=jnp.int32)
    idx = (s[None, :] // sub) * (local * sub) + o_local[:, None] * sub + s[None, :] % sub
    return jnp.take(y, idx.reshape(-1), axis=1)


MESH_ID = pl.DeviceIdType.MESH


def gather_kernel(nrow, ncol, lt_ref, rt_ref, lall_ref, rall_ref, lsend, lrecv, rsend, rrecv, own):
    xh, z = lax.axis_index("xh"), lax.axis_index("z")
    xl, y, core = lax.axis_index("xl"), lax.axis_index("y"), lax.axis_index("core")
    zs, ys = nrow // 2, ncol // 4
    me_r = xh * zs + z
    me_c = (xl * ys + y) * 2 + core
    kl = lt_ref.shape[1]
    kr = rt_ref.shape[1]

    def col_dev(j):
        return (xh, z, j // (ys * 2), (j // 2) % ys, j % 2)

    def row_dev(j):
        return (j // zs, j % zs, xl, y, core)

    barrier = pltpu.get_barrier_semaphore()
    for off in range(1, ncol):
        pl.semaphore_signal(barrier, 1, device_id=col_dev((me_c + off) % ncol), device_id_type=MESH_ID)
    for off in range(1, nrow):
        pl.semaphore_signal(barrier, 1, device_id=row_dev((me_r + off) % nrow), device_id_type=MESH_ID)
    pl.semaphore_wait(barrier, ncol - 1 + nrow - 1)

    lwin = lall_ref.at[:, pl.ds(pl.multiple_of(me_c * kl, 8), kl), :]
    rwin = rall_ref.at[:, pl.ds(pl.multiple_of(me_r * kr, 8), kr), :]
    local_l = pltpu.make_async_copy(lt_ref, lwin, own.at[0])
    local_r = pltpu.make_async_copy(rt_ref, rwin, own.at[1])
    local_l.start()
    local_r.start()
    copies = []
    for off in range(1, max(ncol, nrow)):
        if off < ncol:
            c = pltpu.make_async_remote_copy(
                lt_ref, lwin, lsend.at[off], lrecv.at[off],
                device_id=col_dev((me_c + off) % ncol), device_id_type=MESH_ID)
            c.start()
            copies.append(c)
        if off < nrow:
            c = pltpu.make_async_remote_copy(
                rt_ref, rwin, rsend.at[off], rrecv.at[off],
                device_id=row_dev((me_r + off) % nrow), device_id_type=MESH_ID)
            c.start()
            copies.append(c)
    local_l.wait()
    local_r.wait()
    for c in copies:
        c.wait()


def gather_operands(lt, rt, nrow, ncol):
    b, kl, m = lt.shape
    _, kr, n = rt.shape
    return pl.pallas_call(
        functools.partial(gather_kernel, nrow, ncol),
        out_shape=(
            jax.ShapeDtypeStruct((b, kl * ncol, m), lt.dtype),
            jax.ShapeDtypeStruct((b, kr * nrow, n), rt.dtype),
        ),
        in_specs=[pl.BlockSpec(memory_space=pl.ANY)] * 2,
        out_specs=[pl.BlockSpec(memory_space=pl.ANY)] * 2,
        scratch_shapes=[
            pltpu.SemaphoreType.DMA((ncol,)),
            pltpu.SemaphoreType.DMA((ncol,)),
            pltpu.SemaphoreType.DMA((nrow,)),
            pltpu.SemaphoreType.DMA((nrow,)),
            pltpu.SemaphoreType.DMA((2,)),
        ],
        compiler_params=pltpu.CompilerParams(collective_id=0, has_side_effects=True),
    )(lt, rt)


def body(left, right, prefix_owner, qubit_order):
    row_count = lax.axis_size(ROW)
    col_count = lax.axis_size(COL)
    rows = left.shape[1]
    cols = right.shape[2]
    lp = permute_left(left, prefix_owner, qubit_order, row_count)
    lt = jnp.swapaxes(lp, 1, 2)
    lall, rall = gather_operands(lt, right, row_count, col_count)
    high = lax.Precision.HIGH
    dims = (((0,), (0,)), ((), ()))
    dot = lambda a, b: lax.dot_general(a, b, dims, preferred_element_type=jnp.float32, precision=high)
    t1 = dot(lall[0], rall[0])
    t2 = dot(lall[1], rall[1])
    t3 = dot(lall[0] + lall[1], rall[0] + rall[1])
    tile = jnp.stack([t1 - t2, t3 - t1 - t2], axis=0)
    tile = tile.reshape(2, col_count, rows // col_count, cols)
    out = lax.all_to_all(tile, COL, split_axis=1, concat_axis=3, tiled=True)
    return out.reshape(2, rows // col_count, col_count * cols)


def solution(mesh):
    devices = np.asarray(mesh.devices)
    nr, nc = devices.shape
    fine = Mesh(devices.reshape(2, nr // 2, 2, nc // 4, 2), ("xh", "z", "xl", "y", "core"))
    in_specs = (P(None, ROW, COL), P(None, ROW, COL), P(), P())
    out_specs = P(None, ROW + COL, None)
    return jax.shard_map(body, mesh=fine, in_specs=in_specs, out_specs=out_specs, check_vma=False)
```

```python
import jax
import jax.numpy as jnp
import numpy as np
from jax import lax
from jax.sharding import Mesh
from jax.sharding import PartitionSpec as P

LOW_BITS = 7
PREFIXES = 64

ROW = ("xh", "z")
CHIPS = ("xl", "y")
CORE = "core"
COL = ("xl", "y", "core")


def inverse_owner(prefix_owner, prefixes):
    labels = jnp.arange(prefixes, dtype=jnp.int32)
    match = (prefix_owner[None, :] == labels[:, None]).astype(jnp.int32)
    return jnp.sum(match * labels[None, :], axis=1)


def inner_order(qubit_order, low_bits):
    span = 2**low_bits
    offset = jnp.arange(span, dtype=jnp.int32)
    bits = jnp.bitwise_and(jnp.right_shift(offset[:, None], qubit_order[None, :]), 1)
    powers = jnp.left_shift(jnp.ones((low_bits,), jnp.int32), jnp.arange(low_bits, dtype=jnp.int32))
    return jnp.sum(bits * powers[None, :], axis=1)


def permute_left(left, prefix_owner, qubit_order, row_count):
    _, rows, kcols = left.shape
    span = 2**LOW_BITS
    local = rows // span
    sub = span // row_count
    x = left.reshape(2, local, row_count, sub, kcols)
    x = lax.all_to_all(x, ROW, split_axis=2, concat_axis=2, tiled=True)
    x = x.reshape(2, local * row_count, sub, kcols)
    inv = inverse_owner(prefix_owner, PREFIXES)
    pick = (inv % local) * row_count + inv // local
    y = jnp.take(x, pick, axis=1)
    y = y.reshape(2, row_count, local, sub, kcols)
    y = lax.all_to_all(y, ROW, split_axis=1, concat_axis=1, tiled=True)
    y = y.reshape(2, row_count * local * sub, kcols)
    s = inner_order(qubit_order, LOW_BITS)
    o_local = jnp.arange(local, dtype=jnp.int32)
    idx = (s[None, :] // sub) * (local * sub) + o_local[:, None] * sub + s[None, :] % sub
    return jnp.take(y, idx.reshape(-1), axis=1)


def body(left, right, prefix_owner, qubit_order):
    row_count = lax.axis_size(ROW)
    col_count = lax.axis_size(COL)
    rows = left.shape[1]
    cols = right.shape[2]
    chunks = 4
    width = cols // chunks
    rparts = [right[:, :, j * width:(j + 1) * width] for j in range(chunks)]
    first = lax.all_gather(rparts[0], ROW, axis=1, tiled=True)
    lp = permute_left(left, prefix_owner, qubit_order, row_count)
    lall = lax.all_gather(lp, COL, axis=2, tiled=True)
    rest = lax.optimization_barrier((lall, rparts[1:]))[1]
    gathered = [first] + [lax.all_gather(r, ROW, axis=1, tiled=True) for r in rest]
    lsum = lall[0] + lall[1]
    high = lax.Precision.HIGH
    dot = lambda a, b: jnp.dot(a, b, preferred_element_type=jnp.float32, precision=high)
    outs = []
    for rall in gathered:
        t1 = dot(lall[0], rall[0])
        t2 = dot(lall[1], rall[1])
        t3 = dot(lsum, rall[0] + rall[1])
        tile = jnp.stack([t1 - t2, t3 - t1 - t2], axis=0)
        tile = tile.reshape(2, col_count, rows // col_count, width)
        outs.append(lax.all_to_all(tile, COL, split_axis=1, concat_axis=1, tiled=True))
    out = jnp.stack(outs, axis=3)
    out = jnp.transpose(out, (0, 2, 1, 3, 4))
    return out.reshape(2, rows // col_count, col_count * cols)


def solution(mesh):
    devices = np.asarray(mesh.devices)
    nr, nc = devices.shape
    fine = Mesh(devices.reshape(2, nr // 2, 2, nc // 4, 2), ("xh", "z", "xl", "y", "core"))
    in_specs = (P(None, ROW, COL), P(None, ROW, COL), P(), P())
    out_specs = P(None, ROW + COL, None)
    return jax.shard_map(body, mesh=fine, in_specs=in_specs, out_specs=out_specs, check_vma=False)
```

```python
import jax
import jax.numpy as jnp
import numpy as np
from jax import lax
from jax.sharding import Mesh
from jax.sharding import PartitionSpec as P

LOW_BITS = 7
PREFIXES = 64

ROW = ("xh", "z")
CHIPS = ("xl", "y")
CORE = "core"
COL = ("xl", "y", "core")


def inverse_owner(prefix_owner, prefixes):
    labels = jnp.arange(prefixes, dtype=jnp.int32)
    match = (prefix_owner[None, :] == labels[:, None]).astype(jnp.int32)
    return jnp.sum(match * labels[None, :], axis=1)


def inner_order(qubit_order, low_bits):
    span = 2**low_bits
    offset = jnp.arange(span, dtype=jnp.int32)
    bits = jnp.bitwise_and(jnp.right_shift(offset[:, None], qubit_order[None, :]), 1)
    powers = jnp.left_shift(jnp.ones((low_bits,), jnp.int32), jnp.arange(low_bits, dtype=jnp.int32))
    return jnp.sum(bits * powers[None, :], axis=1)


def permute_left(left, prefix_owner, qubit_order, row_count):
    _, rows, kcols = left.shape
    span = 2**LOW_BITS
    local = rows // span
    sub = span // row_count
    x = left.reshape(2, local, row_count, sub, kcols)
    x = lax.all_to_all(x, ROW, split_axis=2, concat_axis=2, tiled=True)
    x = x.reshape(2, local * row_count, sub, kcols)
    inv = inverse_owner(prefix_owner, PREFIXES)
    pick = (inv % local) * row_count + inv // local
    y = jnp.take(x, pick, axis=1)
    y = y.reshape(2, row_count, local, sub, kcols)
    y = lax.all_to_all(y, ROW, split_axis=1, concat_axis=1, tiled=True)
    y = y.reshape(2, row_count * local * sub, kcols)
    s = inner_order(qubit_order, LOW_BITS)
    o_local = jnp.arange(local, dtype=jnp.int32)
    idx = (s[None, :] // sub) * (local * sub) + o_local[:, None] * sub + s[None, :] % sub
    return jnp.take(y, idx.reshape(-1), axis=1)


def body(left, right, prefix_owner, qubit_order):
    row_count = lax.axis_size(ROW)
    col_count = lax.axis_size(COL)
    rows = left.shape[1]
    cols = right.shape[2]
    rall = lax.all_gather(right, ROW, axis=1, tiled=True)
    lp = permute_left(left, prefix_owner, qubit_order, row_count)
    lp = lax.optimization_barrier((lp, rall))[0]
    lall = lax.all_gather(lp, COL, axis=2, tiled=True)
    high = lax.Precision.HIGH
    dot = lambda a, b: jnp.dot(a, b, preferred_element_type=jnp.float32, precision=high)
    chunks = 2
    width = cols // chunks
    outs = []
    for j in range(chunks):
        rr = rall[:, :, j * width:(j + 1) * width]
        re = dot(lall[0], rr[0]) - dot(lall[1], rr[1])
        im = dot(lall[0], rr[1]) + dot(lall[1], rr[0])
        tile = jnp.stack([re, im], axis=0)
        tile = tile.reshape(2, col_count, rows // col_count, width)
        outs.append(lax.all_to_all(tile, COL, split_axis=1, concat_axis=1, tiled=True))
    out = jnp.stack(outs, axis=3)
    out = jnp.transpose(out, (0, 2, 1, 3, 4))
    return out.reshape(2, rows // col_count, col_count * cols)


def solution(mesh):
    devices = np.asarray(mesh.devices)
    nr, nc = devices.shape
    fine = Mesh(devices.reshape(2, nr // 2, 2, nc // 4, 2), ("xh", "z", "xl", "y", "core"))
    in_specs = (P(None, ROW, COL), P(None, ROW, COL), P(), P())
    out_specs = P(None, ROW + COL, None)
    return jax.shard_map(body, mesh=fine, in_specs=in_specs, out_specs=out_specs, check_vma=False)
```

```python
import jax
import jax.numpy as jnp
import numpy as np
from jax import lax
from jax.sharding import Mesh
from jax.sharding import PartitionSpec as P

LOW_BITS = 7
PREFIXES = 64

ROW = ("xh", "z")
CHIPS = ("xl", "y")
CORE = "core"
COL = ("xl", "y", "core")


def inverse_owner(prefix_owner, prefixes):
    labels = jnp.arange(prefixes, dtype=jnp.int32)
    match = (prefix_owner[None, :] == labels[:, None]).astype(jnp.int32)
    return jnp.sum(match * labels[None, :], axis=1)


def inner_order(qubit_order, low_bits):
    span = 2**low_bits
    offset = jnp.arange(span, dtype=jnp.int32)
    bits = jnp.bitwise_and(jnp.right_shift(offset[:, None], qubit_order[None, :]), 1)
    powers = jnp.left_shift(jnp.ones((low_bits,), jnp.int32), jnp.arange(low_bits, dtype=jnp.int32))
    return jnp.sum(bits * powers[None, :], axis=1)


def permute_left(left, prefix_owner, qubit_order, row_count, col_count):
    _, rows, kcols = left.shape
    span = 2**LOW_BITS
    local = rows // span
    sub = span // row_count
    x = left.reshape(2, local, row_count, sub, kcols)
    x = lax.all_to_all(x, ROW, split_axis=2, concat_axis=2, tiled=True)
    x = x.reshape(2, local * row_count, sub, kcols)
    inv = inverse_owner(prefix_owner, PREFIXES)
    pick = (inv % local) * row_count + inv // local
    y = jnp.take(x, pick, axis=1)
    y = y.reshape(2, row_count, local, sub, kcols)
    y = lax.all_to_all(y, ROW, split_axis=1, concat_axis=1, tiled=True)
    y = y.reshape(2, row_count * local * sub, kcols)
    s = inner_order(qubit_order, LOW_BITS)
    o_local = jnp.arange(local, dtype=jnp.int32)
    idx = (s[None, :] // sub) * (local * sub) + o_local[:, None] * sub + s[None, :] % sub
    idx = idx.reshape(-1)
    q = rows // col_count // 2
    m = jnp.arange(rows, dtype=jnp.int32)
    h, rest = m // (rows // 2), m % (rows // 2)
    pos = (rest // q) * (2 * q) + h * q + rest % q
    return jnp.take(y, jnp.take(idx, pos), axis=1)


def body(left, right, prefix_owner, qubit_order):
    row_count = lax.axis_size(ROW)
    col_count = lax.axis_size(COL)
    rows = left.shape[1]
    cols = right.shape[2]
    rall = lax.all_gather(right, ROW, axis=1, tiled=True)
    lp = permute_left(left, prefix_owner, qubit_order, row_count, col_count)
    lt = jnp.swapaxes(lp, 1, 2)
    halves = 2
    part = rows // halves
    lt = lax.optimization_barrier((lt, rall))[0]
    high = lax.Precision.HIGH
    dims = (((0,), (0,)), ((), ()))
    dot = lambda a, b: lax.dot_general(a, b, dims, preferred_element_type=jnp.float32, precision=high)
    rsum = rall[0] + rall[1]
    outs = []
    prev = None
    for h in range(halves):
        piece = lt[:, :, h * part:(h + 1) * part]
        if prev is not None:
            piece = lax.optimization_barrier((piece, prev))[0]
        lall = lax.all_gather(piece, COL, axis=1, tiled=True)
        prev = lall
        t1 = dot(lall[0], rall[0])
        t2 = dot(lall[1], rall[1])
        t3 = dot(lall[0] + lall[1], rsum)
        tile = jnp.stack([t1 - t2, t3 - t1 - t2], axis=0)
        tile = tile.reshape(2, col_count, part // col_count, cols)
        outs.append(lax.all_to_all(tile, COL, split_axis=1, concat_axis=1, tiled=True))
    out = jnp.stack(outs, axis=1)
    out = jnp.transpose(out, (0, 1, 3, 2, 4))
    return out.reshape(2, rows // col_count, col_count * cols)


def solution(mesh):
    devices = np.asarray(mesh.devices)
    nr, nc = devices.shape
    fine = Mesh(devices.reshape(2, nr // 2, 2, nc // 4, 2), ("xh", "z", "xl", "y", "core"))
    in_specs = (P(None, ROW, COL), P(None, ROW, COL), P(), P())
    out_specs = P(None, ROW + COL, None)
    return jax.shard_map(body, mesh=fine, in_specs=in_specs, out_specs=out_specs, check_vma=False)
```

```python
import jax
import jax.numpy as jnp
import numpy as np
from jax import lax
from jax.sharding import Mesh
from jax.sharding import PartitionSpec as P

LOW_BITS = 7
PREFIXES = 64

ROW = ("xh", "z")
CHIPS = ("xl", "y")
CORE = "core"
COL = ("xl", "y", "core")


def inverse_owner(prefix_owner, prefixes):
    labels = jnp.arange(prefixes, dtype=jnp.int32)
    match = (prefix_owner[None, :] == labels[:, None]).astype(jnp.int32)
    return jnp.sum(match * labels[None, :], axis=1)


def inner_order(qubit_order, low_bits):
    span = 2**low_bits
    offset = jnp.arange(span, dtype=jnp.int32)
    bits = jnp.bitwise_and(jnp.right_shift(offset[:, None], qubit_order[None, :]), 1)
    powers = jnp.left_shift(jnp.ones((low_bits,), jnp.int32), jnp.arange(low_bits, dtype=jnp.int32))
    return jnp.sum(bits * powers[None, :], axis=1)


def permute_left(left, prefix_owner, qubit_order, row_count, col_count):
    _, rows, kcols = left.shape
    span = 2**LOW_BITS
    local = rows // span
    sub = span // row_count
    x = left.reshape(2, local, row_count, sub, kcols)
    x = lax.all_to_all(x, ROW, split_axis=2, concat_axis=2, tiled=True)
    x = x.reshape(2, local * row_count, sub, kcols)
    inv = inverse_owner(prefix_owner, PREFIXES)
    pick = (inv % local) * row_count + inv // local
    y = jnp.take(x, pick, axis=1)
    y = y.reshape(2, row_count, local, sub, kcols)
    y = lax.all_to_all(y, ROW, split_axis=1, concat_axis=1, tiled=True)
    y = y.reshape(2, row_count * local * sub, kcols)
    s = inner_order(qubit_order, LOW_BITS)
    o_local = jnp.arange(local, dtype=jnp.int32)
    idx = (s[None, :] // sub) * (local * sub) + o_local[:, None] * sub + s[None, :] % sub
    idx = idx.reshape(-1)
    q = rows // col_count // 2
    m = jnp.arange(rows, dtype=jnp.int32)
    h, rest = m // (rows // 2), m % (rows // 2)
    pos = (rest // q) * (2 * q) + h * q + rest % q
    return jnp.take(y, jnp.take(idx, pos), axis=1)


def body(left, right, prefix_owner, qubit_order):
    row_count = lax.axis_size(ROW)
    col_count = lax.axis_size(COL)
    rows = left.shape[1]
    cols = right.shape[2]
    rall = lax.all_gather(right, ROW, axis=1, tiled=True)
    lp = permute_left(left, prefix_owner, qubit_order, row_count, col_count)
    lt = jnp.swapaxes(lp, 1, 2)
    halves = 2
    part = rows // halves
    lt = lax.optimization_barrier((lt, rall))[0]
    high = lax.Precision.HIGH
    dims = (((0,), (0,)), ((), ()))
    dot = lambda a, b: lax.dot_general(a, b, dims, preferred_element_type=jnp.float32, precision=high)
    outs = []
    prev = None
    for h in range(halves):
        piece = lt[:, :, h * part:(h + 1) * part]
        if prev is not None:
            piece = lax.optimization_barrier((piece, prev))[0]
        lall = lax.all_gather(piece, COL, axis=1, tiled=True)
        prev = lall
        re = dot(lall[0], rall[0]) - dot(lall[1], rall[1])
        im = dot(lall[0], rall[1]) + dot(lall[1], rall[0])
        tile = jnp.stack([re, im], axis=0)
        tile = tile.reshape(2, col_count, part // col_count, cols)
        outs.append(lax.all_to_all(tile, COL, split_axis=1, concat_axis=3, tiled=True))
    out = jnp.concatenate(outs, axis=1)
    return out.reshape(2, rows // col_count, col_count * cols)


def solution(mesh):
    devices = np.asarray(mesh.devices)
    nr, nc = devices.shape
    fine = Mesh(devices.reshape(2, nr // 2, 2, nc // 4, 2), ("xh", "z", "xl", "y", "core"))
    in_specs = (P(None, ROW, COL), P(None, ROW, COL), P(), P())
    out_specs = P(None, ROW + COL, None)
    return jax.shard_map(body, mesh=fine, in_specs=in_specs, out_specs=out_specs, check_vma=False)
```

```python
import jax
import jax.numpy as jnp
import numpy as np
from jax import lax
from jax.sharding import Mesh
from jax.sharding import PartitionSpec as P

LOW_BITS = 7
PREFIXES = 64

ROW = ("xh", "z")
CHIPS = ("xl", "y")
CORE = "core"
COL = ("xl", "y", "core")


def inverse_owner(prefix_owner, prefixes):
    labels = jnp.arange(prefixes, dtype=jnp.int32)
    match = (prefix_owner[None, :] == labels[:, None]).astype(jnp.int32)
    return jnp.sum(match * labels[None, :], axis=1)


def inner_order(qubit_order, low_bits):
    span = 2**low_bits
    offset = jnp.arange(span, dtype=jnp.int32)
    bits = jnp.bitwise_and(jnp.right_shift(offset[:, None], qubit_order[None, :]), 1)
    powers = jnp.left_shift(jnp.ones((low_bits,), jnp.int32), jnp.arange(low_bits, dtype=jnp.int32))
    return jnp.sum(bits * powers[None, :], axis=1)


def permute_left(left, prefix_owner, qubit_order, row_count, col_count):
    _, rows, kcols = left.shape
    span = 2**LOW_BITS
    local = rows // span
    sub = span // row_count
    x = left.reshape(2, local, row_count, sub, kcols)
    x = lax.all_to_all(x, ROW, split_axis=2, concat_axis=2, tiled=True)
    x = x.reshape(2, local * row_count, sub, kcols)
    inv = inverse_owner(prefix_owner, PREFIXES)
    pick = (inv % local) * row_count + inv // local
    y = jnp.take(x, pick, axis=1)
    y = y.reshape(2, row_count, local, sub, kcols)
    y = lax.all_to_all(y, ROW, split_axis=1, concat_axis=1, tiled=True)
    y = y.reshape(2, row_count * local * sub, kcols)
    s = inner_order(qubit_order, LOW_BITS)
    o_local = jnp.arange(local, dtype=jnp.int32)
    idx = (s[None, :] // sub) * (local * sub) + o_local[:, None] * sub + s[None, :] % sub
    idx = idx.reshape(-1)
    q = rows // col_count // 2
    m = jnp.arange(rows, dtype=jnp.int32)
    h, rest = m // (rows // 2), m % (rows // 2)
    pos = (rest // q) * (2 * q) + h * q + rest % q
    return jnp.take(y, jnp.take(idx, pos), axis=1)


def body(left, right, prefix_owner, qubit_order):
    row_count = lax.axis_size(ROW)
    col_count = lax.axis_size(COL)
    rows = left.shape[1]
    cols = right.shape[2]
    rall = lax.all_gather(right, ROW, axis=1, tiled=True)
    lp = permute_left(left, prefix_owner, qubit_order, row_count, col_count)
    lt = jnp.swapaxes(lp, 1, 2)
    halves = 2
    part = rows // halves
    lt = lax.optimization_barrier((lt, rall))[0]
    high = lax.Precision.HIGH
    dims = (((0,), (0,)), ((), ()))
    dot = lambda a, b: lax.dot_general(a, b, dims, preferred_element_type=jnp.float32, precision=high)
    outs = []
    prev = None
    for h in range(halves):
        piece = lt[:, :, h * part:(h + 1) * part]
        piece = jnp.swapaxes(piece, 0, 1).reshape(piece.shape[1], 2 * part)
        if prev is not None:
            piece = lax.optimization_barrier((piece, prev))[0]
        lall = lax.all_gather(piece, COL, axis=0, tiled=True)
        prev = lall
        pr = dot(lall, rall[0])
        pi = dot(lall, rall[1])
        re = pr[:part] - pi[part:]
        im = pi[:part] + pr[part:]
        tile = jnp.stack([re, im], axis=0)
        tile = tile.reshape(2, col_count, part // col_count, cols)
        outs.append(lax.all_to_all(tile, COL, split_axis=1, concat_axis=3, tiled=True))
    out = jnp.concatenate(outs, axis=1)
    return out.reshape(2, rows // col_count, col_count * cols)


def solution(mesh):
    devices = np.asarray(mesh.devices)
    nr, nc = devices.shape
    fine = Mesh(devices.reshape(2, nr // 2, 2, nc // 4, 2), ("xh", "z", "xl", "y", "core"))
    in_specs = (P(None, ROW, COL), P(None, ROW, COL), P(), P())
    out_specs = P(None, ROW + COL, None)
    return jax.shard_map(body, mesh=fine, in_specs=in_specs, out_specs=out_specs, check_vma=False)
```

```python
import jax
import jax.numpy as jnp
import numpy as np
from jax import lax
from jax.sharding import Mesh
from jax.sharding import PartitionSpec as P

LOW_BITS = 7
PREFIXES = 64

ROW = ("xh", "z")
CHIPS = ("xl", "y")
CORE = "core"
COL = ("xl", "y", "core")


def inverse_owner(prefix_owner, prefixes):
    labels = jnp.arange(prefixes, dtype=jnp.int32)
    match = (prefix_owner[None, :] == labels[:, None]).astype(jnp.int32)
    return jnp.sum(match * labels[None, :], axis=1)


def inner_order(qubit_order, low_bits):
    span = 2**low_bits
    offset = jnp.arange(span, dtype=jnp.int32)
    bits = jnp.bitwise_and(jnp.right_shift(offset[:, None], qubit_order[None, :]), 1)
    powers = jnp.left_shift(jnp.ones((low_bits,), jnp.int32), jnp.arange(low_bits, dtype=jnp.int32))
    return jnp.sum(bits * powers[None, :], axis=1)


def permute_left(left, prefix_owner, qubit_order, row_count, col_count):
    _, rows, kcols = left.shape
    span = 2**LOW_BITS
    local = rows // span
    sub = span // row_count
    x = left.reshape(2, local, row_count, sub, kcols)
    x = lax.all_to_all(x, ROW, split_axis=2, concat_axis=2, tiled=True)
    x = x.reshape(2, local * row_count, sub, kcols)
    inv = inverse_owner(prefix_owner, PREFIXES)
    pick = (inv % local) * row_count + inv // local
    y = jnp.take(x, pick, axis=1)
    y = y.reshape(2, row_count, local, sub, kcols)
    y = lax.all_to_all(y, ROW, split_axis=1, concat_axis=1, tiled=True)
    y = y.reshape(2, row_count * local * sub, kcols)
    s = inner_order(qubit_order, LOW_BITS)
    o_local = jnp.arange(local, dtype=jnp.int32)
    idx = (s[None, :] // sub) * (local * sub) + o_local[:, None] * sub + s[None, :] % sub
    idx = idx.reshape(-1)
    return jnp.take(y, jnp.take(idx, part_order(rows, col_count)), axis=1)


def part_sizes(q_total):
    return [q_total // 2, q_total // 4, q_total - q_total // 2 - q_total // 4]


def part_order(rows, col_count):
    q_total = rows // col_count
    pos = []
    off = 0
    for qp in part_sizes(q_total):
        for c in range(col_count):
            pos.extend(c * q_total + off + i for i in range(qp))
        off += qp
    return np.asarray(pos, np.int32)


def body(left, right, prefix_owner, qubit_order):
    row_count = lax.axis_size(ROW)
    col_count = lax.axis_size(COL)
    rows = left.shape[1]
    cols = right.shape[2]
    rall = lax.all_gather(right, ROW, axis=1, tiled=True)
    lp = permute_left(left, prefix_owner, qubit_order, row_count, col_count)
    lt = jnp.swapaxes(lp, 1, 2)
    lt = lax.optimization_barrier((lt, rall))[0]
    high = lax.Precision.HIGH
    dims = (((0,), (0,)), ((), ()))
    dot = lambda a, b: lax.dot_general(a, b, dims, preferred_element_type=jnp.float32, precision=high)
    outs = []
    prev = None
    start = 0
    for qp in part_sizes(rows // col_count):
        part = qp * col_count
        piece = lt[:, :, start:start + part]
        start += part
        piece = jnp.swapaxes(piece, 0, 1).reshape(piece.shape[1], 2 * part)
        if prev is not None:
            piece = lax.optimization_barrier((piece, prev))[0]
        lall = lax.all_gather(piece, COL, axis=0, tiled=True)
        prev = lall
        pr = dot(lall, rall[0])
        pi = dot(lall, rall[1])
        re = pr[:part] - pi[part:]
        im = pi[:part] + pr[part:]
        tile = jnp.stack([re, im], axis=0)
        tile = tile.reshape(2, col_count, qp, cols)
        outs.append(lax.all_to_all(tile, COL, split_axis=1, concat_axis=3, tiled=True))
    out = jnp.concatenate(outs, axis=2)
    return out.reshape(2, rows // col_count, col_count * cols)


def solution(mesh):
    devices = np.asarray(mesh.devices)
    nr, nc = devices.shape
    fine = Mesh(devices.reshape(2, nr // 2, 2, nc // 4, 2), ("xh", "z", "xl", "y", "core"))
    in_specs = (P(None, ROW, COL), P(None, ROW, COL), P(), P())
    out_specs = P(None, ROW + COL, None)
    return jax.shard_map(body, mesh=fine, in_specs=in_specs, out_specs=out_specs, check_vma=False)
```

```python
import jax
import jax.numpy as jnp
import numpy as np
from jax import lax
from jax.sharding import Mesh
from jax.sharding import PartitionSpec as P

LOW_BITS = 7
PREFIXES = 64

ROW = ("xh", "z")
CHIPS = ("xl", "y")
CORE = "core"
COL = ("xl", "y", "core")


def inverse_owner(prefix_owner, prefixes):
    labels = jnp.arange(prefixes, dtype=jnp.int32)
    match = (prefix_owner[None, :] == labels[:, None]).astype(jnp.int32)
    return jnp.sum(match * labels[None, :], axis=1)


def inner_order(qubit_order, low_bits):
    span = 2**low_bits
    offset = jnp.arange(span, dtype=jnp.int32)
    bits = jnp.bitwise_and(jnp.right_shift(offset[:, None], qubit_order[None, :]), 1)
    powers = jnp.left_shift(jnp.ones((low_bits,), jnp.int32), jnp.arange(low_bits, dtype=jnp.int32))
    return jnp.sum(bits * powers[None, :], axis=1)


def permute_left(left, prefix_owner, qubit_order, row_count, col_count):
    _, rows, kcols = left.shape
    span = 2**LOW_BITS
    local = rows // span
    sub = span // row_count
    x = left.reshape(2, local, row_count, sub, kcols)
    x = lax.all_to_all(x, ROW, split_axis=2, concat_axis=2, tiled=True)
    x = x.reshape(2, local * row_count, sub, kcols)
    inv = inverse_owner(prefix_owner, PREFIXES)
    pick = (inv % local) * row_count + inv // local
    y = jnp.take(x, pick, axis=1)
    y = y.reshape(2, row_count, local, sub, kcols)
    y = lax.all_to_all(y, ROW, split_axis=1, concat_axis=1, tiled=True)
    y = y.reshape(2, row_count * local * sub, kcols)
    s = inner_order(qubit_order, LOW_BITS)
    o_local = jnp.arange(local, dtype=jnp.int32)
    idx = (s[None, :] // sub) * (local * sub) + o_local[:, None] * sub + s[None, :] % sub
    idx = idx.reshape(-1)
    return jnp.take(y, jnp.take(idx, part_order(rows, col_count)), axis=1)


def part_sizes(q_total):
    return [q_total * 3 // 4, q_total - q_total * 3 // 4]


def part_order(rows, col_count):
    q_total = rows // col_count
    pos = []
    off = 0
    for qp in part_sizes(q_total):
        for c in range(col_count):
            pos.extend(c * q_total + off + i for i in range(qp))
        off += qp
    return np.asarray(pos, np.int32)


def body(left, right, prefix_owner, qubit_order):
    row_count = lax.axis_size(ROW)
    col_count = lax.axis_size(COL)
    rows = left.shape[1]
    cols = right.shape[2]
    rall = lax.all_gather(right, ROW, axis=1, tiled=True)
    lp = permute_left(left, prefix_owner, qubit_order, row_count, col_count)
    lt = jnp.swapaxes(lp, 1, 2)
    lt = lax.optimization_barrier((lt, rall))[0]
    high = lax.Precision.HIGH
    dims = (((0,), (0,)), ((), ()))
    dot = lambda a, b: lax.dot_general(a, b, dims, preferred_element_type=jnp.float32, precision=high)
    outs = []
    prev = None
    start = 0
    for qp in part_sizes(rows // col_count):
        part = qp * col_count
        piece = lt[:, :, start:start + part]
        start += part
        piece = jnp.swapaxes(piece, 0, 1).reshape(piece.shape[1], 2 * part)
        if prev is not None:
            piece = lax.optimization_barrier((piece, prev))[0]
        lall = lax.all_gather(piece, COL, axis=0, tiled=True)
        prev = lall
        pr = dot(lall, rall[0])
        pi = dot(lall, rall[1])
        re = pr[:part] - pi[part:]
        im = pi[:part] + pr[part:]
        tile = jnp.stack([re, im], axis=0)
        tile = tile.reshape(2, col_count, qp, cols)
        outs.append(lax.all_to_all(tile, COL, split_axis=1, concat_axis=3, tiled=True))
    out = jnp.concatenate(outs, axis=2)
    return out.reshape(2, rows // col_count, col_count * cols)


def solution(mesh):
    devices = np.asarray(mesh.devices)
    nr, nc = devices.shape
    fine = Mesh(devices.reshape(2, nr // 2, 2, nc // 4, 2), ("xh", "z", "xl", "y", "core"))
    in_specs = (P(None, ROW, COL), P(None, ROW, COL), P(), P())
    out_specs = P(None, ROW + COL, None)
    return jax.shard_map(body, mesh=fine, in_specs=in_specs, out_specs=out_specs, check_vma=False)
```

```python
import jax
import jax.numpy as jnp
import numpy as np
from jax import lax
from jax.sharding import Mesh
from jax.sharding import PartitionSpec as P

LOW_BITS = 7
PREFIXES = 64

ROW = ("xh", "z")
CHIPS = ("xl", "y")
CORE = "core"
COL = ("xl", "y", "core")


def inverse_owner(prefix_owner, prefixes):
    labels = jnp.arange(prefixes, dtype=jnp.int32)
    match = (prefix_owner[None, :] == labels[:, None]).astype(jnp.int32)
    return jnp.sum(match * labels[None, :], axis=1)


def inner_order(qubit_order, low_bits):
    span = 2**low_bits
    offset = jnp.arange(span, dtype=jnp.int32)
    bits = jnp.bitwise_and(jnp.right_shift(offset[:, None], qubit_order[None, :]), 1)
    powers = jnp.left_shift(jnp.ones((low_bits,), jnp.int32), jnp.arange(low_bits, dtype=jnp.int32))
    return jnp.sum(bits * powers[None, :], axis=1)


def permute_left(left, prefix_owner, qubit_order, row_count, col_count):
    _, rows, kcols = left.shape
    span = 2**LOW_BITS
    local = rows // span
    sub = span // row_count
    x = left.reshape(2, local, row_count, sub, kcols)
    x = lax.all_to_all(x, ROW, split_axis=2, concat_axis=2, tiled=True)
    x = x.reshape(2, local * row_count, sub, kcols)
    inv = inverse_owner(prefix_owner, PREFIXES)
    pick = (inv % local) * row_count + inv // local
    y = jnp.take(x, pick, axis=1)
    y = y.reshape(2, row_count, local, sub, kcols)
    y = lax.all_to_all(y, ROW, split_axis=1, concat_axis=1, tiled=True)
    y = y.reshape(2, row_count * local * sub, kcols)
    s = inner_order(qubit_order, LOW_BITS)
    o_local = jnp.arange(local, dtype=jnp.int32)
    idx = (s[None, :] // sub) * (local * sub) + o_local[:, None] * sub + s[None, :] % sub
    idx = idx.reshape(-1)
    return jnp.take(y, jnp.take(idx, part_order(rows, col_count)), axis=1)


def part_sizes(q_total):
    return [q_total * 3 // 4, q_total - q_total * 3 // 4]


def part_order(rows, col_count):
    q_total = rows // col_count
    pos = []
    off = 0
    for qp in part_sizes(q_total):
        for c in range(col_count):
            pos.extend(c * q_total + off + i for i in range(qp))
        off += qp
    return np.asarray(pos, np.int32)


def body(left, right, prefix_owner, qubit_order):
    row_count = lax.axis_size(ROW)
    col_count = lax.axis_size(COL)
    rows = left.shape[1]
    cols = right.shape[2]
    rall = lax.all_gather(right, ROW, axis=1, tiled=True)
    lp = permute_left(left, prefix_owner, qubit_order, row_count, col_count)
    lt = jnp.swapaxes(lp, 1, 2)
    lt = lax.optimization_barrier((lt, rall))[0]
    dims = (((0,), (0,)), ((), ()))
    dot = lambda a, b: lax.dot_general(a, b, dims, preferred_element_type=jnp.float32)

    def split(a):
        hi = lax.reduce_precision(a, exponent_bits=8, mantissa_bits=7)
        return hi.astype(jnp.bfloat16), (a - hi).astype(jnp.bfloat16)

    rcat = jnp.concatenate([rall[0], rall[1]], axis=1)
    r_hi, r_lo = split(rcat)
    outs = []
    prev = None
    start = 0
    for qp in part_sizes(rows // col_count):
        part = qp * col_count
        piece = lt[:, :, start:start + part]
        start += part
        piece = jnp.swapaxes(piece, 0, 1).reshape(piece.shape[1], 2 * part)
        if prev is not None:
            piece = lax.optimization_barrier((piece, prev))[0]
        lall = lax.all_gather(piece, COL, axis=0, tiled=True)
        prev = lall
        l_hi, l_lo = split(lall)
        q = dot(l_hi, r_hi) + dot(l_hi, r_lo) + dot(l_lo, r_hi)
        re = q[:part, :cols] - q[part:, cols:]
        im = q[:part, cols:] + q[part:, :cols]
        tile = jnp.stack([re, im], axis=0)
        tile = tile.reshape(2, col_count, qp, cols)
        outs.append(lax.all_to_all(tile, COL, split_axis=1, concat_axis=3, tiled=True))
    out = jnp.concatenate(outs, axis=2)
    return out.reshape(2, rows // col_count, col_count * cols)


def solution(mesh):
    devices = np.asarray(mesh.devices)
    nr, nc = devices.shape
    fine = Mesh(devices.reshape(2, nr // 2, 2, nc // 4, 2), ("xh", "z", "xl", "y", "core"))
    in_specs = (P(None, ROW, COL), P(None, ROW, COL), P(), P())
    out_specs = P(None, ROW + COL, None)
    return jax.shard_map(body, mesh=fine, in_specs=in_specs, out_specs=out_specs, check_vma=False)
```

```python
import jax
import jax.numpy as jnp
import numpy as np
from jax import lax
from jax.sharding import Mesh
from jax.sharding import PartitionSpec as P

LOW_BITS = 7
PREFIXES = 64

ROW = ("xh", "z")
CHIPS = ("xl", "y")
CORE = "core"
COL = ("xl", "y", "core")


def inverse_owner(prefix_owner, prefixes):
    labels = jnp.arange(prefixes, dtype=jnp.int32)
    match = (prefix_owner[None, :] == labels[:, None]).astype(jnp.int32)
    return jnp.sum(match * labels[None, :], axis=1)


def inner_order(qubit_order, low_bits):
    span = 2**low_bits
    offset = jnp.arange(span, dtype=jnp.int32)
    bits = jnp.bitwise_and(jnp.right_shift(offset[:, None], qubit_order[None, :]), 1)
    powers = jnp.left_shift(jnp.ones((low_bits,), jnp.int32), jnp.arange(low_bits, dtype=jnp.int32))
    return jnp.sum(bits * powers[None, :], axis=1)


def permute_left(left, prefix_owner, qubit_order, row_count, col_count):
    _, rows, kcols = left.shape
    span = 2**LOW_BITS
    local = rows // span
    sub = span // row_count
    x = left.reshape(2, local, row_count, sub, kcols)
    x = lax.all_to_all(x, ROW, split_axis=2, concat_axis=2, tiled=True)
    x = x.reshape(2, local * row_count, sub, kcols)
    inv = inverse_owner(prefix_owner, PREFIXES)
    pick = (inv % local) * row_count + inv // local
    y = jnp.take(x, pick, axis=1)
    y = y.reshape(2, row_count, local, sub, kcols)
    y = lax.all_to_all(y, ROW, split_axis=1, concat_axis=1, tiled=True)
    y = y.reshape(2, row_count * local * sub, kcols)
    s = inner_order(qubit_order, LOW_BITS)
    o_local = jnp.arange(local, dtype=jnp.int32)
    idx = (s[None, :] // sub) * (local * sub) + o_local[:, None] * sub + s[None, :] % sub
    idx = idx.reshape(-1)
    return jnp.take(y, jnp.take(idx, part_order(rows, col_count)), axis=1)


def part_sizes(q_total):
    return [q_total * 3 // 4, q_total - q_total * 3 // 4]


def part_order(rows, col_count):
    q_total = rows // col_count
    pos = []
    off = 0
    for qp in part_sizes(q_total):
        for c in range(col_count):
            pos.extend(c * q_total + off + i for i in range(qp))
        off += qp
    return np.asarray(pos, np.int32)


def body(left, right, prefix_owner, qubit_order):
    row_count = lax.axis_size(ROW)
    col_count = lax.axis_size(COL)
    rows = left.shape[1]
    cols = right.shape[2]
    rpiece = jnp.swapaxes(right, 0, 1).reshape(right.shape[1], 2 * cols)
    rall = lax.all_gather(rpiece, ROW, axis=0, tiled=True)
    lp = permute_left(left, prefix_owner, qubit_order, row_count, col_count)
    lt = jnp.swapaxes(lp, 1, 2)
    lt = lax.optimization_barrier((lt, rall))[0]
    high = lax.Precision.HIGH
    dims = (((0,), (0,)), ((), ()))
    dot = lambda a, b: lax.dot_general(a, b, dims, preferred_element_type=jnp.float32, precision=high)
    outs = []
    prev = None
    start = 0
    for qp in part_sizes(rows // col_count):
        part = qp * col_count
        piece = lt[:, :, start:start + part]
        start += part
        piece = jnp.swapaxes(piece, 0, 1).reshape(piece.shape[1], 2 * part)
        if prev is not None:
            piece = lax.optimization_barrier((piece, prev))[0]
        lall = lax.all_gather(piece, COL, axis=0, tiled=True)
        prev = lall
        q = dot(lall, rall)
        re = q[:part, :cols] - q[part:, cols:]
        im = q[:part, cols:] + q[part:, :cols]
        tile = jnp.stack([re, im], axis=0)
        tile = tile.reshape(2, col_count, qp, cols)
        outs.append(lax.all_to_all(tile, COL, split_axis=1, concat_axis=3, tiled=True))
    out = jnp.concatenate(outs, axis=2)
    return out.reshape(2, rows // col_count, col_count * cols)


def solution(mesh):
    devices = np.asarray(mesh.devices)
    nr, nc = devices.shape
    fine = Mesh(devices.reshape(2, nr // 2, 2, nc // 4, 2), ("xh", "z", "xl", "y", "core"))
    in_specs = (P(None, ROW, COL), P(None, ROW, COL), P(), P())
    out_specs = P(None, ROW + COL, None)
    return jax.shard_map(body, mesh=fine, in_specs=in_specs, out_specs=out_specs, check_vma=False)
```

```python
import jax
import jax.numpy as jnp
import numpy as np
from jax import lax
from jax.sharding import Mesh
from jax.sharding import PartitionSpec as P

LOW_BITS = 7
PREFIXES = 64

ROW = ("xh", "z")
CHIPS = ("xl", "y")
CORE = "core"
COL = ("xl", "y", "core")


def inverse_owner(prefix_owner, prefixes):
    labels = jnp.arange(prefixes, dtype=jnp.int32)
    match = (prefix_owner[None, :] == labels[:, None]).astype(jnp.int32)
    return jnp.sum(match * labels[None, :], axis=1)


def inner_order(qubit_order, low_bits):
    span = 2**low_bits
    offset = jnp.arange(span, dtype=jnp.int32)
    bits = jnp.bitwise_and(jnp.right_shift(offset[:, None], qubit_order[None, :]), 1)
    powers = jnp.left_shift(jnp.ones((low_bits,), jnp.int32), jnp.arange(low_bits, dtype=jnp.int32))
    return jnp.sum(bits * powers[None, :], axis=1)


def permute_left(left, prefix_owner, qubit_order, row_count, col_count):
    _, rows, kcols = left.shape
    span = 2**LOW_BITS
    local = rows // span
    sub = span // row_count
    x = left.reshape(2, local, row_count, sub, kcols)
    x = lax.all_to_all(x, ROW, split_axis=2, concat_axis=2, tiled=True)
    x = x.reshape(2, local * row_count, sub, kcols)
    inv = inverse_owner(prefix_owner, PREFIXES)
    pick = (inv % local) * row_count + inv // local
    y = jnp.take(x, pick, axis=1)
    y = y.reshape(2, row_count, local, sub, kcols)
    y = lax.all_to_all(y, ROW, split_axis=1, concat_axis=1, tiled=True)
    y = y.reshape(2, row_count * local * sub, kcols)
    s = inner_order(qubit_order, LOW_BITS)
    o_local = jnp.arange(local, dtype=jnp.int32)
    idx = (s[None, :] // sub) * (local * sub) + o_local[:, None] * sub + s[None, :] % sub
    idx = idx.reshape(-1)
    return jnp.take(y, jnp.take(idx, part_order(rows, col_count)), axis=1)


def part_sizes(q_total):
    return [q_total * 3 // 4, q_total - q_total * 3 // 4]


def part_order(rows, col_count):
    q_total = rows // col_count
    pos = []
    off = 0
    for qp in part_sizes(q_total):
        for c in range(col_count):
            pos.extend(c * q_total + off + i for i in range(qp))
        off += qp
    return np.asarray(pos, np.int32)


def body(left, right, prefix_owner, qubit_order):
    row_count = lax.axis_size(ROW)
    col_count = lax.axis_size(COL)
    rows = left.shape[1]
    cols = right.shape[2]
    splits = 2
    sub = cols // splits
    rpiece = jnp.transpose(right.reshape(2, right.shape[1], splits, sub), (1, 2, 0, 3))
    rpiece = rpiece.reshape(right.shape[1], 2 * cols)
    rall = lax.all_gather(rpiece, ROW, axis=0, tiled=True)
    lp = permute_left(left, prefix_owner, qubit_order, row_count, col_count)
    lt = jnp.swapaxes(lp, 1, 2)
    lt = lax.optimization_barrier((lt, rall))[0]
    high = lax.Precision.HIGH
    dims = (((0,), (0,)), ((), ()))
    dot = lambda a, b: lax.dot_general(a, b, dims, preferred_element_type=jnp.float32, precision=high)
    outs = []
    prev = None
    start = 0
    for p, qp in enumerate(part_sizes(rows // col_count)):
        part = qp * col_count
        piece = lt[:, :, start:start + part]
        start += part
        piece = jnp.swapaxes(piece, 0, 1).reshape(piece.shape[1], 2 * part)
        if prev is not None:
            piece = lax.optimization_barrier((piece, prev))[0]
        lall = lax.all_gather(piece, COL, axis=0, tiled=True)
        prev = lall
        pieces = []
        nsplit = splits if p == 0 else 1
        step = splits // nsplit
        for j in range(nsplit):
            q = dot(lall, rall[:, j * step * 2 * sub:(j + 1) * step * 2 * sub])
            q = q.reshape(2 * part, step, 2, sub)
            re = q[:part, :, 0] - q[part:, :, 1]
            im = q[:part, :, 1] + q[part:, :, 0]
            tile = jnp.stack([re, im], axis=0)
            tile = tile.reshape(2, col_count, qp, step * sub)
            got = lax.all_to_all(tile, COL, split_axis=1, concat_axis=3, tiled=True)
            pieces.append(got.reshape(2, qp, col_count, step, sub))
        got = jnp.concatenate(pieces, axis=3) if nsplit > 1 else pieces[0]
        outs.append(got.reshape(2, 1, qp, col_count * cols))
    out = jnp.concatenate(outs, axis=2)
    return out.reshape(2, rows // col_count, col_count * cols)


def solution(mesh):
    devices = np.asarray(mesh.devices)
    nr, nc = devices.shape
    fine = Mesh(devices.reshape(2, nr // 2, 2, nc // 4, 2), ("xh", "z", "xl", "y", "core"))
    in_specs = (P(None, ROW, COL), P(None, ROW, COL), P(), P())
    out_specs = P(None, ROW + COL, None)
    return jax.shard_map(body, mesh=fine, in_specs=in_specs, out_specs=out_specs, check_vma=False)
```

```python
import functools

import jax
import jax.numpy as jnp
import numpy as np
from jax import lax
from jax.experimental import pallas as pl
from jax.experimental.pallas import tpu as pltpu
from jax.sharding import Mesh
from jax.sharding import PartitionSpec as P

LOW_BITS = 7
PREFIXES = 64

ROW = ("xh", "z")
CHIPS = ("xl", "y")
CORE = "core"
COL = ("xl", "y", "core")


def inverse_owner(prefix_owner, prefixes):
    labels = jnp.arange(prefixes, dtype=jnp.int32)
    match = (prefix_owner[None, :] == labels[:, None]).astype(jnp.int32)
    return jnp.sum(match * labels[None, :], axis=1)


def inner_order(qubit_order, low_bits):
    span = 2**low_bits
    offset = jnp.arange(span, dtype=jnp.int32)
    bits = jnp.bitwise_and(jnp.right_shift(offset[:, None], qubit_order[None, :]), 1)
    powers = jnp.left_shift(jnp.ones((low_bits,), jnp.int32), jnp.arange(low_bits, dtype=jnp.int32))
    return jnp.sum(bits * powers[None, :], axis=1)


def permute_left(left, prefix_owner, qubit_order, row_count, col_count):
    _, rows, kcols = left.shape
    span = 2**LOW_BITS
    local = rows // span
    sub = span // row_count
    x = left.reshape(2, local, row_count, sub, kcols)
    x = lax.all_to_all(x, ROW, split_axis=2, concat_axis=2, tiled=True)
    x = x.reshape(2, local * row_count, sub, kcols)
    inv = inverse_owner(prefix_owner, PREFIXES)
    pick = (inv % local) * row_count + inv // local
    y = jnp.take(x, pick, axis=1)
    y = y.reshape(2, row_count, local, sub, kcols)
    y = lax.all_to_all(y, ROW, split_axis=1, concat_axis=1, tiled=True)
    y = y.reshape(2, row_count * local * sub, kcols)
    s = inner_order(qubit_order, LOW_BITS)
    o_local = jnp.arange(local, dtype=jnp.int32)
    idx = (s[None, :] // sub) * (local * sub) + o_local[:, None] * sub + s[None, :] % sub
    idx = idx.reshape(-1)
    return jnp.take(y, jnp.take(idx, part_order(rows, col_count)), axis=1)


def part_sizes(q_total):
    return [q_total * 3 // 4, q_total - q_total * 3 // 4]


def part_order(rows, col_count):
    q_total = rows // col_count
    pos = []
    off = 0
    for qp in part_sizes(q_total):
        for c in range(col_count):
            pos.extend(c * q_total + off + i for i in range(qp))
        off += qp
    return np.asarray(pos, np.int32)


MESH_ID = pl.DeviceIdType.MESH


def scatter_kernel(ncol, tile_ref, out_ref, send, recv, own):
    xh, z = lax.axis_index("xh"), lax.axis_index("z")
    xl, y, core = lax.axis_index("xl"), lax.axis_index("y"), lax.axis_index("core")
    ys = ncol // 4
    me = (xl * ys + y) * 2 + core
    w = tile_ref.shape[-1]

    def col_dev(j):
        return (xh, z, j // (ys * 2), (j // 2) % ys, j % 2)

    barrier = pltpu.get_barrier_semaphore()
    for off in range(1, ncol):
        pl.semaphore_signal(barrier, 1, device_id=col_dev((me + off) % ncol), device_id_type=MESH_ID)
    pl.semaphore_wait(barrier, ncol - 1)

    dst = out_ref.at[:, :, pl.ds(pl.multiple_of(me * w, w), w)]
    local = pltpu.make_async_copy(tile_ref.at[me], dst, own.at[0])
    local.start()
    copies = []
    for off in range(1, ncol):
        j = (me + off) % ncol
        c = pltpu.make_async_remote_copy(
            tile_ref.at[j], dst, send.at[off], recv.at[off],
            device_id=col_dev(j), device_id_type=MESH_ID)
        c.start()
        copies.append(c)
    local.wait()
    for c in copies:
        c.wait()


def scatter_cols(tile, ncol):
    _, b, q, w = tile.shape
    return pl.pallas_call(
        functools.partial(scatter_kernel, ncol),
        out_shape=jax.ShapeDtypeStruct((b, q, ncol * w), tile.dtype),
        in_specs=[pl.BlockSpec(memory_space=pl.ANY)],
        out_specs=pl.BlockSpec(memory_space=pl.ANY),
        scratch_shapes=[
            pltpu.SemaphoreType.DMA((ncol,)),
            pltpu.SemaphoreType.DMA((ncol,)),
            pltpu.SemaphoreType.DMA((1,)),
        ],
        compiler_params=pltpu.CompilerParams(collective_id=0, has_side_effects=True),
    )(tile)


def body(left, right, prefix_owner, qubit_order):
    row_count = lax.axis_size(ROW)
    col_count = lax.axis_size(COL)
    rows = left.shape[1]
    cols = right.shape[2]
    rpiece = jnp.swapaxes(right, 0, 1).reshape(right.shape[1], 2 * cols)
    rall = lax.all_gather(rpiece, ROW, axis=0, tiled=True)
    lp = permute_left(left, prefix_owner, qubit_order, row_count, col_count)
    lt = jnp.swapaxes(lp, 1, 2)
    lt = lax.optimization_barrier((lt, rall))[0]
    high = lax.Precision.HIGH
    dims = (((0,), (0,)), ((), ()))
    dot = lambda a, b: lax.dot_general(a, b, dims, preferred_element_type=jnp.float32, precision=high)
    outs = []
    prev = None
    start = 0
    for qp in part_sizes(rows // col_count):
        part = qp * col_count
        piece = lt[:, :, start:start + part]
        start += part
        piece = jnp.swapaxes(piece, 0, 1).reshape(piece.shape[1], 2 * part)
        if prev is not None:
            piece = lax.optimization_barrier((piece, prev))[0]
        lall = lax.all_gather(piece, COL, axis=0, tiled=True)
        prev = lall
        q = dot(lall, rall)
        re = q[:part, :cols] - q[part:, cols:]
        im = q[:part, cols:] + q[part:, :cols]
        if start == rows:
            tile = jnp.stack([re.reshape(col_count, qp, cols), im.reshape(col_count, qp, cols)], axis=1)
            outs.append(scatter_cols(tile, col_count).reshape(2, 1, qp, col_count * cols))
        else:
            tile = jnp.stack([re, im], axis=0)
            tile = tile.reshape(2, col_count, qp, cols)
            outs.append(lax.all_to_all(tile, COL, split_axis=1, concat_axis=3, tiled=True))
    out = jnp.concatenate(outs, axis=2)
    return out.reshape(2, rows // col_count, col_count * cols)


def solution(mesh):
    devices = np.asarray(mesh.devices)
    nr, nc = devices.shape
    fine = Mesh(devices.reshape(2, nr // 2, 2, nc // 4, 2), ("xh", "z", "xl", "y", "core"))
    in_specs = (P(None, ROW, COL), P(None, ROW, COL), P(), P())
    out_specs = P(None, ROW + COL, None)
    return jax.shard_map(body, mesh=fine, in_specs=in_specs, out_specs=out_specs, check_vma=False)
```

```python
import functools

import jax
import jax.numpy as jnp
import numpy as np
from jax import lax
from jax.experimental import pallas as pl
from jax.experimental.pallas import tpu as pltpu
from jax.sharding import Mesh
from jax.sharding import PartitionSpec as P

LOW_BITS = 7
PREFIXES = 64

ROW = ("xh", "z")
CHIPS = ("xl", "y")
CORE = "core"
COL = ("xl", "y", "core")


def inverse_owner(prefix_owner, prefixes):
    labels = jnp.arange(prefixes, dtype=jnp.int32)
    match = (prefix_owner[None, :] == labels[:, None]).astype(jnp.int32)
    return jnp.sum(match * labels[None, :], axis=1)


def inner_order(qubit_order, low_bits):
    span = 2**low_bits
    offset = jnp.arange(span, dtype=jnp.int32)
    bits = jnp.bitwise_and(jnp.right_shift(offset[:, None], qubit_order[None, :]), 1)
    powers = jnp.left_shift(jnp.ones((low_bits,), jnp.int32), jnp.arange(low_bits, dtype=jnp.int32))
    return jnp.sum(bits * powers[None, :], axis=1)


def permute_left(left, prefix_owner, qubit_order, row_count, col_count):
    _, rows, kcols = left.shape
    span = 2**LOW_BITS
    local = rows // span
    sub = span // row_count
    x = left.reshape(2, local, row_count, sub, kcols)
    x = lax.all_to_all(x, ROW, split_axis=2, concat_axis=2, tiled=True)
    x = x.reshape(2, local * row_count, sub, kcols)
    inv = inverse_owner(prefix_owner, PREFIXES)
    pick = (inv % local) * row_count + inv // local
    y = jnp.take(x, pick, axis=1)
    y = y.reshape(2, row_count, local, sub, kcols)
    y = lax.all_to_all(y, ROW, split_axis=1, concat_axis=1, tiled=True)
    y = y.reshape(2, row_count * local * sub, kcols)
    s = inner_order(qubit_order, LOW_BITS)
    o_local = jnp.arange(local, dtype=jnp.int32)
    idx = (s[None, :] // sub) * (local * sub) + o_local[:, None] * sub + s[None, :] % sub
    idx = idx.reshape(-1)
    return jnp.take(y, jnp.take(idx, part_order(rows, col_count)), axis=1)


def part_sizes(q_total):
    return [q_total * 3 // 4, q_total - q_total * 3 // 4]


def part_order(rows, col_count):
    q_total = rows // col_count
    pos = []
    off = 0
    for qp in part_sizes(q_total):
        for c in range(col_count):
            pos.extend(c * q_total + off + i for i in range(qp))
        off += qp
    return np.asarray(pos, np.int32)


MESH_ID = pl.DeviceIdType.MESH


def scatter_kernel(ncol, tile_ref, out_ref, send, recv, own):
    xh, z = lax.axis_index("xh"), lax.axis_index("z")
    xl, y, core = lax.axis_index("xl"), lax.axis_index("y"), lax.axis_index("core")
    ys = ncol // 4
    me = (xl * ys + y) * 2 + core
    w = tile_ref.shape[-1]

    def col_dev(j):
        return (xh, z, j // (ys * 2), (j // 2) % ys, j % 2)

    barrier = pltpu.get_barrier_semaphore()
    for off in range(1, ncol):
        pl.semaphore_signal(barrier, 1, device_id=col_dev((me + off) % ncol), device_id_type=MESH_ID)
    pl.semaphore_wait(barrier, ncol - 1)

    dst = out_ref.at[:, :, pl.ds(pl.multiple_of(me * w, w), w)]
    local = pltpu.make_async_copy(tile_ref.at[me], dst, own.at[0])
    local.start()
    copies = []
    for off in range(1, ncol):
        j = (me + off) % ncol
        c = pltpu.make_async_remote_copy(
            tile_ref.at[j], dst, send.at[off], recv.at[off],
            device_id=col_dev(j), device_id_type=MESH_ID)
        c.start()
        copies.append(c)
    local.wait()
    for c in copies:
        c.wait()


def scatter_cols(tile, ncol, cid):
    _, b, q, w = tile.shape
    return pl.pallas_call(
        functools.partial(scatter_kernel, ncol),
        out_shape=jax.ShapeDtypeStruct((b, q, ncol * w), tile.dtype),
        in_specs=[pl.BlockSpec(memory_space=pl.ANY)],
        out_specs=pl.BlockSpec(memory_space=pl.ANY),
        scratch_shapes=[
            pltpu.SemaphoreType.DMA((ncol,)),
            pltpu.SemaphoreType.DMA((ncol,)),
            pltpu.SemaphoreType.DMA((1,)),
        ],
        compiler_params=pltpu.CompilerParams(collective_id=cid, has_side_effects=True),
    )(tile)


def body(left, right, prefix_owner, qubit_order):
    row_count = lax.axis_size(ROW)
    col_count = lax.axis_size(COL)
    rows = left.shape[1]
    cols = right.shape[2]
    rpiece = jnp.swapaxes(right, 0, 1).reshape(right.shape[1], 2 * cols)
    rall = lax.all_gather(rpiece, ROW, axis=0, tiled=True)
    lp = permute_left(left, prefix_owner, qubit_order, row_count, col_count)
    lt = jnp.swapaxes(lp, 1, 2)
    lt = lax.optimization_barrier((lt, rall))[0]
    high = lax.Precision.HIGH
    dims = (((0,), (0,)), ((), ()))
    dot = lambda a, b: lax.dot_general(a, b, dims, preferred_element_type=jnp.float32, precision=high)
    outs = []
    prev = None
    start = 0
    for qp in part_sizes(rows // col_count):
        part = qp * col_count
        piece = lt[:, :, start:start + part]
        start += part
        piece = jnp.swapaxes(piece, 0, 1).reshape(piece.shape[1], 2 * part)
        if prev is not None:
            piece = lax.optimization_barrier((piece, prev))[0]
        lall = lax.all_gather(piece, COL, axis=0, tiled=True)
        prev = lall
        q = dot(lall, rall)
        re = q[:part, :cols] - q[part:, cols:]
        im = q[:part, cols:] + q[part:, :cols]
        tile = jnp.stack([re.reshape(col_count, qp, cols), im.reshape(col_count, qp, cols)], axis=1)
        outs.append(scatter_cols(tile, col_count, len(outs)).reshape(2, 1, qp, col_count * cols))
    out = jnp.concatenate(outs, axis=2)
    return out.reshape(2, rows // col_count, col_count * cols)


def solution(mesh):
    devices = np.asarray(mesh.devices)
    nr, nc = devices.shape
    fine = Mesh(devices.reshape(2, nr // 2, 2, nc // 4, 2), ("xh", "z", "xl", "y", "core"))
    in_specs = (P(None, ROW, COL), P(None, ROW, COL), P(), P())
    out_specs = P(None, ROW + COL, None)
    return jax.shard_map(body, mesh=fine, in_specs=in_specs, out_specs=out_specs, check_vma=False)
```

```python
import functools

import jax
import jax.numpy as jnp
import numpy as np
from jax import lax
from jax.experimental import pallas as pl
from jax.experimental.pallas import tpu as pltpu
from jax.sharding import Mesh
from jax.sharding import PartitionSpec as P

LOW_BITS = 7
PREFIXES = 64

ROW = ("xh", "z")
CHIPS = ("xl", "y")
CORE = "core"
COL = ("xl", "y", "core")


def inverse_owner(prefix_owner, prefixes):
    labels = jnp.arange(prefixes, dtype=jnp.int32)
    match = (prefix_owner[None, :] == labels[:, None]).astype(jnp.int32)
    return jnp.sum(match * labels[None, :], axis=1)


def inner_order(qubit_order, low_bits):
    span = 2**low_bits
    offset = jnp.arange(span, dtype=jnp.int32)
    bits = jnp.bitwise_and(jnp.right_shift(offset[:, None], qubit_order[None, :]), 1)
    powers = jnp.left_shift(jnp.ones((low_bits,), jnp.int32), jnp.arange(low_bits, dtype=jnp.int32))
    return jnp.sum(bits * powers[None, :], axis=1)


def permute_left(left, prefix_owner, qubit_order, row_count, col_count):
    _, rows, kcols = left.shape
    span = 2**LOW_BITS
    local = rows // span
    sub = span // row_count
    x = left.reshape(2, local, row_count, sub, kcols)
    x = lax.all_to_all(x, ROW, split_axis=2, concat_axis=2, tiled=True)
    x = x.reshape(2, local * row_count, sub, kcols)
    inv = inverse_owner(prefix_owner, PREFIXES)
    pick = (inv % local) * row_count + inv // local
    y = jnp.take(x, pick, axis=1)
    y = y.reshape(2, row_count, local, sub, kcols)
    y = lax.all_to_all(y, ROW, split_axis=1, concat_axis=1, tiled=True)
    y = y.reshape(2, row_count * local * sub, kcols)
    s = inner_order(qubit_order, LOW_BITS)
    o_local = jnp.arange(local, dtype=jnp.int32)
    idx = (s[None, :] // sub) * (local * sub) + o_local[:, None] * sub + s[None, :] % sub
    idx = idx.reshape(-1)
    return jnp.take(y, jnp.take(idx, part_order(rows, col_count)), axis=1)


def part_sizes(q_total):
    return [q_total * 5 // 8, q_total - q_total * 5 // 8]


def part_order(rows, col_count):
    q_total = rows // col_count
    pos = []
    off = 0
    for qp in part_sizes(q_total):
        for c in range(col_count):
            pos.extend(c * q_total + off + i for i in range(qp))
        off += qp
    return np.asarray(pos, np.int32)


MESH_ID = pl.DeviceIdType.MESH


def scatter_kernel(ncol, tile_ref, out_ref, send, recv, own):
    xh, z = lax.axis_index("xh"), lax.axis_index("z")
    xl, y, core = lax.axis_index("xl"), lax.axis_index("y"), lax.axis_index("core")
    ys = ncol // 4
    me = (xl * ys + y) * 2 + core
    w = tile_ref.shape[-1]

    def col_dev(j):
        return (xh, z, j // (ys * 2), (j // 2) % ys, j % 2)

    barrier = pltpu.get_barrier_semaphore()
    for off in range(1, ncol):
        pl.semaphore_signal(barrier, 1, device_id=col_dev((me + off) % ncol), device_id_type=MESH_ID)
    pl.semaphore_wait(barrier, ncol - 1)

    dst = out_ref.at[:, :, pl.ds(pl.multiple_of(me * w, w), w)]
    local = pltpu.make_async_copy(tile_ref.at[me], dst, own.at[0])
    local.start()
    copies = []
    for off in range(1, ncol):
        j = (me + off) % ncol
        c = pltpu.make_async_remote_copy(
            tile_ref.at[j], dst, send.at[off], recv.at[off],
            device_id=col_dev(j), device_id_type=MESH_ID)
        c.start()
        copies.append(c)
    local.wait()
    for c in copies:
        c.wait()


def scatter_cols(tile, ncol):
    _, b, q, w = tile.shape
    return pl.pallas_call(
        functools.partial(scatter_kernel, ncol),
        out_shape=jax.ShapeDtypeStruct((b, q, ncol * w), tile.dtype),
        in_specs=[pl.BlockSpec(memory_space=pl.ANY)],
        out_specs=pl.BlockSpec(memory_space=pl.ANY),
        scratch_shapes=[
            pltpu.SemaphoreType.DMA((ncol,)),
            pltpu.SemaphoreType.DMA((ncol,)),
            pltpu.SemaphoreType.DMA((1,)),
        ],
        compiler_params=pltpu.CompilerParams(collective_id=0, has_side_effects=True),
    )(tile)


def body(left, right, prefix_owner, qubit_order):
    row_count = lax.axis_size(ROW)
    col_count = lax.axis_size(COL)
    rows = left.shape[1]
    cols = right.shape[2]
    rpiece = jnp.swapaxes(right, 0, 1).reshape(right.shape[1], 2 * cols)
    rall = lax.all_gather(rpiece, ROW, axis=0, tiled=True)
    lp = permute_left(left, prefix_owner, qubit_order, row_count, col_count)
    lt = jnp.swapaxes(lp, 1, 2)
    lt = lax.optimization_barrier((lt, rall))[0]
    high = lax.Precision.HIGH
    dims = (((0,), (0,)), ((), ()))
    dot = lambda a, b: lax.dot_general(a, b, dims, preferred_element_type=jnp.float32, precision=high)
    outs = []
    prev = None
    start = 0
    for qp in part_sizes(rows // col_count):
        part = qp * col_count
        piece = lt[:, :, start:start + part]
        start += part
        piece = jnp.swapaxes(piece, 0, 1).reshape(piece.shape[1], 2 * part)
        if prev is not None:
            piece = lax.optimization_barrier((piece, prev))[0]
        lall = lax.all_gather(piece, COL, axis=0, tiled=True)
        prev = lall
        q = dot(lall, rall)
        re = q[:part, :cols] - q[part:, cols:]
        im = q[:part, cols:] + q[part:, :cols]
        if start == rows:
            tile = jnp.stack([re.reshape(col_count, qp, cols), im.reshape(col_count, qp, cols)], axis=1)
            outs.append(scatter_cols(tile, col_count).reshape(2, 1, qp, col_count * cols))
        else:
            tile = jnp.stack([re, im], axis=0)
            tile = tile.reshape(2, col_count, qp, cols)
            outs.append(lax.all_to_all(tile, COL, split_axis=1, concat_axis=3, tiled=True))
    out = jnp.concatenate(outs, axis=2)
    return out.reshape(2, rows // col_count, col_count * cols)


def solution(mesh):
    devices = np.asarray(mesh.devices)
    nr, nc = devices.shape
    fine = Mesh(devices.reshape(2, nr // 2, 2, nc // 4, 2), ("xh", "z", "xl", "y", "core"))
    in_specs = (P(None, ROW, COL), P(None, ROW, COL), P(), P())
    out_specs = P(None, ROW + COL, None)
    return jax.shard_map(body, mesh=fine, in_specs=in_specs, out_specs=out_specs, check_vma=False)
```

```python
import functools

import jax
import jax.numpy as jnp
import numpy as np
from jax import lax
from jax.experimental import pallas as pl
from jax.experimental.pallas import tpu as pltpu
from jax.sharding import Mesh
from jax.sharding import PartitionSpec as P

LOW_BITS = 7
PREFIXES = 64

ROW = ("xh", "z")
CHIPS = ("xl", "y")
CORE = "core"
COL = ("xl", "y", "core")


def inverse_owner(prefix_owner, prefixes):
    labels = jnp.arange(prefixes, dtype=jnp.int32)
    match = (prefix_owner[None, :] == labels[:, None]).astype(jnp.int32)
    return jnp.sum(match * labels[None, :], axis=1)


def inner_order(qubit_order, low_bits):
    span = 2**low_bits
    offset = jnp.arange(span, dtype=jnp.int32)
    bits = jnp.bitwise_and(jnp.right_shift(offset[:, None], qubit_order[None, :]), 1)
    powers = jnp.left_shift(jnp.ones((low_bits,), jnp.int32), jnp.arange(low_bits, dtype=jnp.int32))
    return jnp.sum(bits * powers[None, :], axis=1)


def permute_left(left, prefix_owner, qubit_order, row_count, col_count):
    _, rows, kcols = left.shape
    span = 2**LOW_BITS
    local = rows // span
    sub = span // row_count
    x = left.reshape(2, local, row_count, sub, kcols)
    x = lax.all_to_all(x, ROW, split_axis=2, concat_axis=2, tiled=True)
    x = x.reshape(2, local * row_count, sub, kcols)
    inv = inverse_owner(prefix_owner, PREFIXES)
    pick = (inv % local) * row_count + inv // local
    y = jnp.take(x, pick, axis=1)
    y = y.reshape(2, row_count, local, sub, kcols)
    y = lax.all_to_all(y, ROW, split_axis=1, concat_axis=1, tiled=True)
    y = y.reshape(2, row_count * local * sub, kcols)
    s = inner_order(qubit_order, LOW_BITS)
    o_local = jnp.arange(local, dtype=jnp.int32)
    idx = (s[None, :] // sub) * (local * sub) + o_local[:, None] * sub + s[None, :] % sub
    idx = idx.reshape(-1)
    return jnp.take(y, jnp.take(idx, part_order(rows, col_count)), axis=1)


def part_sizes(q_total):
    return [q_total * 3 // 4, q_total - q_total * 3 // 4]


def part_order(rows, col_count):
    q_total = rows // col_count
    pos = []
    off = 0
    for qp in part_sizes(q_total):
        for c in range(col_count):
            pos.extend(c * q_total + off + i for i in range(qp))
        off += qp
    return np.asarray(pos, np.int32)


MESH_ID = pl.DeviceIdType.MESH


def scatter_kernel(ncol, tile_ref, out_ref, send, recv, own):
    xh, z = lax.axis_index("xh"), lax.axis_index("z")
    xl, y, core = lax.axis_index("xl"), lax.axis_index("y"), lax.axis_index("core")
    ys = ncol // 4
    me = (xl * ys + y) * 2 + core
    w = tile_ref.shape[-1]

    def col_dev(j):
        return (xh, z, j // (ys * 2), (j // 2) % ys, j % 2)

    barrier = pltpu.get_barrier_semaphore()
    for off in range(1, ncol):
        pl.semaphore_signal(barrier, 1, device_id=col_dev((me + off) % ncol), device_id_type=MESH_ID)
    pl.semaphore_wait(barrier, ncol - 1)

    dst = out_ref.at[:, :, pl.ds(pl.multiple_of(me * w, w), w)]
    local = pltpu.make_async_copy(tile_ref.at[me], dst, own.at[0])
    local.start()
    copies = []
    for off in range(1, ncol):
        j = (me + off) % ncol
        c = pltpu.make_async_remote_copy(
            tile_ref.at[j], dst, send.at[off], recv.at[off],
            device_id=col_dev(j), device_id_type=MESH_ID)
        c.start()
        copies.append(c)
    local.wait()
    for c in copies:
        c.wait()


def scatter_cols(tile, ncol):
    _, b, q, w = tile.shape
    return pl.pallas_call(
        functools.partial(scatter_kernel, ncol),
        out_shape=jax.ShapeDtypeStruct((b, q, ncol * w), tile.dtype),
        in_specs=[pl.BlockSpec(memory_space=pl.ANY)],
        out_specs=pl.BlockSpec(memory_space=pl.ANY),
        scratch_shapes=[
            pltpu.SemaphoreType.DMA((ncol,)),
            pltpu.SemaphoreType.DMA((ncol,)),
            pltpu.SemaphoreType.DMA((1,)),
        ],
        compiler_params=pltpu.CompilerParams(collective_id=0, has_side_effects=True),
    )(tile)


def body(left, right, prefix_owner, qubit_order):
    row_count = lax.axis_size(ROW)
    col_count = lax.axis_size(COL)
    rows = left.shape[1]
    cols = right.shape[2]
    rpiece = jnp.swapaxes(right, 0, 1).reshape(right.shape[1], 2 * cols)
    rall = lax.all_gather(rpiece, ROW, axis=0, tiled=True)
    lp = permute_left(left, prefix_owner, qubit_order, row_count, col_count)
    lt = jnp.swapaxes(lp, 1, 2)
    lt = lax.optimization_barrier((lt, rall))[0]
    high = lax.Precision.HIGH
    dims = (((0,), (0,)), ((), ()))
    dot = lambda a, b: lax.dot_general(a, b, dims, preferred_element_type=jnp.float32, precision=high)
    outs = []
    prev = None
    start = 0
    for qp in part_sizes(rows // col_count):
        part = qp * col_count
        piece = lt[:, :, start:start + part]
        start += part
        piece = jnp.swapaxes(piece, 0, 1).reshape(piece.shape[1], 2 * part)
        if prev is not None:
            piece = lax.optimization_barrier((piece, prev))[0]
        lall = lax.all_gather(piece, COL, axis=0, tiled=True)
        prev = lall
        q = dot(lall, rall)
        re = q[:part, :cols] - q[part:, cols:]
        im = q[:part, cols:] + q[part:, :cols]
        outs.append(jnp.stack([re.reshape(col_count, qp, cols), im.reshape(col_count, qp, cols)], axis=1))
    tile = jnp.concatenate(outs, axis=2)
    return scatter_cols(tile, col_count)


def solution(mesh):
    devices = np.asarray(mesh.devices)
    nr, nc = devices.shape
    fine = Mesh(devices.reshape(2, nr // 2, 2, nc // 4, 2), ("xh", "z", "xl", "y", "core"))
    in_specs = (P(None, ROW, COL), P(None, ROW, COL), P(), P())
    out_specs = P(None, ROW + COL, None)
    return jax.shard_map(body, mesh=fine, in_specs=in_specs, out_specs=out_specs, check_vma=False)
```

```python
import functools

import jax
import jax.numpy as jnp
import numpy as np
from jax import lax
from jax.experimental import pallas as pl
from jax.experimental.pallas import tpu as pltpu
from jax.sharding import Mesh
from jax.sharding import PartitionSpec as P

LOW_BITS = 7
PREFIXES = 64

ROW = ("xh", "z")
CHIPS = ("xl", "y")
CORE = "core"
COL = ("xl", "y", "core")


def inverse_owner(prefix_owner, prefixes):
    labels = jnp.arange(prefixes, dtype=jnp.int32)
    match = (prefix_owner[None, :] == labels[:, None]).astype(jnp.int32)
    return jnp.sum(match * labels[None, :], axis=1)


def inner_order(qubit_order, low_bits):
    span = 2**low_bits
    offset = jnp.arange(span, dtype=jnp.int32)
    bits = jnp.bitwise_and(jnp.right_shift(offset[:, None], qubit_order[None, :]), 1)
    powers = jnp.left_shift(jnp.ones((low_bits,), jnp.int32), jnp.arange(low_bits, dtype=jnp.int32))
    return jnp.sum(bits * powers[None, :], axis=1)


def permute_left(left, prefix_owner, qubit_order, row_count, col_count):
    _, rows, kcols = left.shape
    span = 2**LOW_BITS
    local = rows // span
    sub = span // row_count
    x = left.reshape(2, local, row_count, sub, kcols)
    x = lax.all_to_all(x, ROW, split_axis=2, concat_axis=2, tiled=True)
    x = x.reshape(2, local * row_count, sub, kcols)
    inv = inverse_owner(prefix_owner, PREFIXES)
    pick = (inv % local) * row_count + inv // local
    y = jnp.take(x, pick, axis=1)
    y = y.reshape(2, row_count, local, sub, kcols)
    y = lax.all_to_all(y, ROW, split_axis=1, concat_axis=1, tiled=True)
    y = y.reshape(2, row_count * local * sub, kcols)
    s = inner_order(qubit_order, LOW_BITS)
    o_local = jnp.arange(local, dtype=jnp.int32)
    idx = (s[None, :] // sub) * (local * sub) + o_local[:, None] * sub + s[None, :] % sub
    idx = idx.reshape(-1)
    return jnp.take(y, jnp.take(idx, part_order(rows, col_count)), axis=1)


def part_sizes(q_total):
    return [q_total * 3 // 4, q_total - q_total * 3 // 4]


def part_order(rows, col_count):
    q_total = rows // col_count
    pos = []
    off = 0
    for qp in part_sizes(q_total):
        for c in range(col_count):
            pos.extend(c * q_total + off + i for i in range(qp))
        off += qp
    return np.asarray(pos, np.int32)


MESH_ID = pl.DeviceIdType.MESH


def scatter_kernel(ncol, tile_ref, out_ref, send, recv, own):
    xh, z = lax.axis_index("xh"), lax.axis_index("z")
    xl, y, core = lax.axis_index("xl"), lax.axis_index("y"), lax.axis_index("core")
    ys = ncol // 4
    me = (xl * ys + y) * 2 + core
    w = tile_ref.shape[-1]

    def col_dev(j):
        return (xh, z, j // (ys * 2), (j // 2) % ys, j % 2)

    barrier = pltpu.get_barrier_semaphore()
    for off in range(1, ncol):
        pl.semaphore_signal(barrier, 1, device_id=col_dev((me + off) % ncol), device_id_type=MESH_ID)
    pl.semaphore_wait(barrier, ncol - 1)

    dst = out_ref.at[:, :, pl.ds(pl.multiple_of(me * w, w), w)]
    local = pltpu.make_async_copy(tile_ref.at[me], dst, own.at[0])
    local.start()
    copies = []
    for off in range(1, ncol):
        j = (me + off) % ncol
        c = pltpu.make_async_remote_copy(
            tile_ref.at[j], dst, send.at[off], recv.at[off],
            device_id=col_dev(j), device_id_type=MESH_ID)
        c.start()
        copies.append(c)
    local.wait()
    for c in copies:
        c.wait()


def scatter_cols(tile, ncol):
    _, b, q, w = tile.shape
    return pl.pallas_call(
        functools.partial(scatter_kernel, ncol),
        out_shape=jax.ShapeDtypeStruct((b, q, ncol * w), tile.dtype),
        in_specs=[pl.BlockSpec(memory_space=pl.ANY)],
        out_specs=pl.BlockSpec(memory_space=pl.ANY),
        scratch_shapes=[
            pltpu.SemaphoreType.DMA((ncol,)),
            pltpu.SemaphoreType.DMA((ncol,)),
            pltpu.SemaphoreType.DMA((1,)),
        ],
        compiler_params=pltpu.CompilerParams(collective_id=0, has_side_effects=True),
    )(tile)


def body(left, right, prefix_owner, qubit_order):
    row_count = lax.axis_size(ROW)
    col_count = lax.axis_size(COL)
    rows = left.shape[1]
    cols = right.shape[2]
    rpiece = jnp.swapaxes(right, 0, 1).reshape(right.shape[1], 2 * cols)
    rall = lax.all_gather(rpiece, ROW, axis=0, tiled=True)
    lp = permute_left(left, prefix_owner, qubit_order, row_count, col_count)
    lt = jnp.swapaxes(lp, 1, 2)
    lt = lax.optimization_barrier((lt, rall))[0]
    high = lax.Precision.HIGH
    dims = (((0,), (0,)), ((), ()))
    dot = lambda a, b: lax.dot_general(a, b, dims, preferred_element_type=jnp.float32, precision=high)
    outs = []
    prev = None
    start = 0
    for qp in part_sizes(rows // col_count):
        part = qp * col_count
        piece = lt[:, :, start:start + part]
        start += part
        piece = jnp.swapaxes(piece, 0, 1).reshape(piece.shape[1], 2 * part)
        if prev is not None:
            piece = lax.optimization_barrier((piece, prev))[0]
        lall = lax.all_gather(piece, COL, axis=0, tiled=True)
        prev = lall
        q = dot(lall, rall)
        re = q[:part, :cols] - q[part:, cols:]
        im = q[:part, cols:] + q[part:, :cols]
        if start == rows:
            tile = jnp.stack([re.reshape(col_count, qp, cols), im.reshape(col_count, qp, cols)], axis=1)
            outs.append(scatter_cols(tile, col_count).reshape(2, 1, qp, col_count * cols))
        else:
            tile = jnp.stack([re, im], axis=0)
            tile = tile.reshape(2, col_count, qp, cols)
            got = lax.all_to_all(tile, COL, split_axis=1, concat_axis=1, tiled=True)
            outs.append(jnp.swapaxes(got, 1, 2).reshape(2, 1, qp, col_count * cols))
    out = jnp.concatenate(outs, axis=2)
    return out.reshape(2, rows // col_count, col_count * cols)


def solution(mesh):
    devices = np.asarray(mesh.devices)
    nr, nc = devices.shape
    fine = Mesh(devices.reshape(2, nr // 2, 2, nc // 4, 2), ("xh", "z", "xl", "y", "core"))
    in_specs = (P(None, ROW, COL), P(None, ROW, COL), P(), P())
    out_specs = P(None, ROW + COL, None)
    return jax.shard_map(body, mesh=fine, in_specs=in_specs, out_specs=out_specs, check_vma=False)
```

```python
import functools

import jax
import jax.numpy as jnp
import numpy as np
from jax import lax
from jax.experimental import pallas as pl
from jax.experimental.pallas import tpu as pltpu
from jax.sharding import Mesh
from jax.sharding import PartitionSpec as P

LOW_BITS = 7
PREFIXES = 64

ROW = ("xh", "z")
CHIPS = ("xl", "y")
CORE = "core"
COL = ("xl", "y", "core")


def inverse_owner(prefix_owner, prefixes):
    labels = jnp.arange(prefixes, dtype=jnp.int32)
    match = (prefix_owner[None, :] == labels[:, None]).astype(jnp.int32)
    return jnp.sum(match * labels[None, :], axis=1)


def inner_order(qubit_order, low_bits):
    span = 2**low_bits
    offset = jnp.arange(span, dtype=jnp.int32)
    bits = jnp.bitwise_and(jnp.right_shift(offset[:, None], qubit_order[None, :]), 1)
    powers = jnp.left_shift(jnp.ones((low_bits,), jnp.int32), jnp.arange(low_bits, dtype=jnp.int32))
    return jnp.sum(bits * powers[None, :], axis=1)


def permute_left(left, prefix_owner, qubit_order, row_count, col_count):
    _, rows, kcols = left.shape
    span = 2**LOW_BITS
    local = rows // span
    sub = span // row_count
    x = left.reshape(2, local, row_count, sub, kcols)
    x = lax.all_to_all(x, ROW, split_axis=2, concat_axis=2, tiled=True)
    x = x.reshape(2, local * row_count, sub, kcols)
    inv = inverse_owner(prefix_owner, PREFIXES)
    pick = (inv % local) * row_count + inv // local
    y = jnp.take(x, pick, axis=1)
    y = y.reshape(2, row_count, local, sub, kcols)
    y = lax.all_to_all(y, ROW, split_axis=1, concat_axis=1, tiled=True)
    y = y.reshape(2, row_count * local * sub, kcols)
    s = inner_order(qubit_order, LOW_BITS)
    o_local = jnp.arange(local, dtype=jnp.int32)
    idx = (s[None, :] // sub) * (local * sub) + o_local[:, None] * sub + s[None, :] % sub
    idx = idx.reshape(-1)
    return jnp.take(y, jnp.take(idx, part_order(rows, col_count)), axis=1)


def part_sizes(q_total):
    return [q_total * 13 // 16, q_total - q_total * 13 // 16]


def part_order(rows, col_count):
    q_total = rows // col_count
    pos = []
    off = 0
    for qp in part_sizes(q_total):
        for c in range(col_count):
            pos.extend(c * q_total + off + i for i in range(qp))
        off += qp
    return np.asarray(pos, np.int32)


MESH_ID = pl.DeviceIdType.MESH


def scatter_kernel(ncol, tile_ref, out_ref, send, recv, own):
    xh, z = lax.axis_index("xh"), lax.axis_index("z")
    xl, y, core = lax.axis_index("xl"), lax.axis_index("y"), lax.axis_index("core")
    ys = ncol // 4
    me = (xl * ys + y) * 2 + core
    w = tile_ref.shape[-1]

    def col_dev(j):
        return (xh, z, j // (ys * 2), (j // 2) % ys, j % 2)

    barrier = pltpu.get_barrier_semaphore()
    for off in range(1, ncol):
        pl.semaphore_signal(barrier, 1, device_id=col_dev((me + off) % ncol), device_id_type=MESH_ID)
    pl.semaphore_wait(barrier, ncol - 1)

    dst = out_ref.at[:, :, pl.ds(pl.multiple_of(me * w, w), w)]
    local = pltpu.make_async_copy(tile_ref.at[me], dst, own.at[0])
    local.start()
    copies = []
    for off in range(1, ncol):
        j = (me + off) % ncol
        c = pltpu.make_async_remote_copy(
            tile_ref.at[j], dst, send.at[off], recv.at[off],
            device_id=col_dev(j), device_id_type=MESH_ID)
        c.start()
        copies.append(c)
    local.wait()
    for c in copies:
        c.wait()


def scatter_cols(tile, ncol):
    _, b, q, w = tile.shape
    return pl.pallas_call(
        functools.partial(scatter_kernel, ncol),
        out_shape=jax.ShapeDtypeStruct((b, q, ncol * w), tile.dtype),
        in_specs=[pl.BlockSpec(memory_space=pl.ANY)],
        out_specs=pl.BlockSpec(memory_space=pl.ANY),
        scratch_shapes=[
            pltpu.SemaphoreType.DMA((ncol,)),
            pltpu.SemaphoreType.DMA((ncol,)),
            pltpu.SemaphoreType.DMA((1,)),
        ],
        compiler_params=pltpu.CompilerParams(collective_id=0, has_side_effects=True),
    )(tile)


def body(left, right, prefix_owner, qubit_order):
    row_count = lax.axis_size(ROW)
    col_count = lax.axis_size(COL)
    rows = left.shape[1]
    cols = right.shape[2]
    rpiece = jnp.swapaxes(right, 0, 1).reshape(right.shape[1], 2 * cols)
    rall = lax.all_gather(rpiece, ROW, axis=0, tiled=True)
    lp = permute_left(left, prefix_owner, qubit_order, row_count, col_count)
    lt = jnp.swapaxes(lp, 1, 2)
    lt = lax.optimization_barrier((lt, rall))[0]
    high = lax.Precision.HIGH
    dims = (((0,), (0,)), ((), ()))
    dot = lambda a, b: lax.dot_general(a, b, dims, preferred_element_type=jnp.float32, precision=high)
    outs = []
    prev = None
    start = 0
    for qp in part_sizes(rows // col_count):
        part = qp * col_count
        piece = lt[:, :, start:start + part]
        start += part
        piece = jnp.swapaxes(piece, 0, 1).reshape(piece.shape[1], 2 * part)
        if prev is not None:
            piece = lax.optimization_barrier((piece, prev))[0]
        lall = lax.all_gather(piece, COL, axis=0, tiled=True)
        prev = lall
        q = dot(lall, rall)
        re = q[:part, :cols] - q[part:, cols:]
        im = q[:part, cols:] + q[part:, :cols]
        if start == rows:
            tile = jnp.stack([re.reshape(col_count, qp, cols), im.reshape(col_count, qp, cols)], axis=1)
            outs.append(scatter_cols(tile, col_count).reshape(2, 1, qp, col_count * cols))
        else:
            tile = jnp.stack([re, im], axis=0)
            tile = tile.reshape(2, col_count, qp, cols)
            outs.append(lax.all_to_all(tile, COL, split_axis=1, concat_axis=3, tiled=True))
    out = jnp.concatenate(outs, axis=2)
    return out.reshape(2, rows // col_count, col_count * cols)


def solution(mesh):
    devices = np.asarray(mesh.devices)
    nr, nc = devices.shape
    fine = Mesh(devices.reshape(2, nr // 2, 2, nc // 4, 2), ("xh", "z", "xl", "y", "core"))
    in_specs = (P(None, ROW, COL), P(None, ROW, COL), P(), P())
    out_specs = P(None, ROW + COL, None)
    return jax.shard_map(body, mesh=fine, in_specs=in_specs, out_specs=out_specs, check_vma=False)
```

```python
import functools

import jax
import jax.numpy as jnp
import numpy as np
from jax import lax
from jax.experimental import pallas as pl
from jax.experimental.pallas import tpu as pltpu
from jax.sharding import Mesh
from jax.sharding import PartitionSpec as P

LOW_BITS = 7
PREFIXES = 64

ROW = ("xh", "z")
CHIPS = ("xl", "y")
CORE = "core"
COL = ("xl", "y", "core")


def inverse_owner(prefix_owner, prefixes):
    labels = jnp.arange(prefixes, dtype=jnp.int32)
    match = (prefix_owner[None, :] == labels[:, None]).astype(jnp.int32)
    return jnp.sum(match * labels[None, :], axis=1)


def inner_order(qubit_order, low_bits):
    span = 2**low_bits
    offset = jnp.arange(span, dtype=jnp.int32)
    bits = jnp.bitwise_and(jnp.right_shift(offset[:, None], qubit_order[None, :]), 1)
    powers = jnp.left_shift(jnp.ones((low_bits,), jnp.int32), jnp.arange(low_bits, dtype=jnp.int32))
    return jnp.sum(bits * powers[None, :], axis=1)


def permute_left(left, prefix_owner, qubit_order, row_count, col_count):
    _, rows, kcols = left.shape
    span = 2**LOW_BITS
    local = rows // span
    sub = span // row_count
    x = left.reshape(2, local, row_count, sub, kcols)
    x = lax.all_to_all(x, ROW, split_axis=2, concat_axis=2, tiled=True)
    x = x.reshape(2, local * row_count, sub, kcols)
    inv = inverse_owner(prefix_owner, PREFIXES)
    pick = (inv % local) * row_count + inv // local
    y = jnp.take(x, pick, axis=1)
    y = y.reshape(2, row_count, local, sub, kcols)
    y = lax.all_to_all(y, ROW, split_axis=1, concat_axis=1, tiled=True)
    y = y.reshape(2, row_count * local * sub, kcols)
    s = inner_order(qubit_order, LOW_BITS)
    o_local = jnp.arange(local, dtype=jnp.int32)
    idx = (s[None, :] // sub) * (local * sub) + o_local[:, None] * sub + s[None, :] % sub
    idx = idx.reshape(-1)
    return jnp.take(y, jnp.take(idx, part_order(rows, col_count)), axis=1)


def part_sizes(q_total):
    return [q_total * 7 // 8, q_total - q_total * 7 // 8]


def part_order(rows, col_count):
    q_total = rows // col_count
    pos = []
    off = 0
    for qp in part_sizes(q_total):
        for c in range(col_count):
            pos.extend(c * q_total + off + i for i in range(qp))
        off += qp
    return np.asarray(pos, np.int32)


MESH_ID = pl.DeviceIdType.MESH


def scatter_kernel(ncol, tile_ref, out_ref, send, recv, own):
    xh, z = lax.axis_index("xh"), lax.axis_index("z")
    xl, y, core = lax.axis_index("xl"), lax.axis_index("y"), lax.axis_index("core")
    ys = ncol // 4
    me = (xl * ys + y) * 2 + core
    w = tile_ref.shape[-1]

    def col_dev(j):
        return (xh, z, j // (ys * 2), (j // 2) % ys, j % 2)

    barrier = pltpu.get_barrier_semaphore()
    for off in range(1, ncol):
        pl.semaphore_signal(barrier, 1, device_id=col_dev((me + off) % ncol), device_id_type=MESH_ID)
    pl.semaphore_wait(barrier, ncol - 1)

    dst = out_ref.at[:, :, pl.ds(pl.multiple_of(me * w, w), w)]
    local = pltpu.make_async_copy(tile_ref.at[me], dst, own.at[0])
    local.start()
    copies = []
    for off in range(1, ncol):
        j = (me + off) % ncol
        c = pltpu.make_async_remote_copy(
            tile_ref.at[j], dst, send.at[off], recv.at[off],
            device_id=col_dev(j), device_id_type=MESH_ID)
        c.start()
        copies.append(c)
    local.wait()
    for c in copies:
        c.wait()


def scatter_cols(tile, ncol):
    _, b, q, w = tile.shape
    return pl.pallas_call(
        functools.partial(scatter_kernel, ncol),
        out_shape=jax.ShapeDtypeStruct((b, q, ncol * w), tile.dtype),
        in_specs=[pl.BlockSpec(memory_space=pl.ANY)],
        out_specs=pl.BlockSpec(memory_space=pl.ANY),
        scratch_shapes=[
            pltpu.SemaphoreType.DMA((ncol,)),
            pltpu.SemaphoreType.DMA((ncol,)),
            pltpu.SemaphoreType.DMA((1,)),
        ],
        compiler_params=pltpu.CompilerParams(collective_id=0, has_side_effects=True),
    )(tile)


def body(left, right, prefix_owner, qubit_order):
    row_count = lax.axis_size(ROW)
    col_count = lax.axis_size(COL)
    rows = left.shape[1]
    cols = right.shape[2]
    rpiece = jnp.swapaxes(right, 0, 1).reshape(right.shape[1], 2 * cols)
    rall = lax.all_gather(rpiece, ROW, axis=0, tiled=True)
    lp = permute_left(left, prefix_owner, qubit_order, row_count, col_count)
    lt = jnp.swapaxes(lp, 1, 2)
    lt = lax.optimization_barrier((lt, rall))[0]
    high = lax.Precision.HIGH
    dims = (((0,), (0,)), ((), ()))
    dot = lambda a, b: lax.dot_general(a, b, dims, preferred_element_type=jnp.float32, precision=high)
    outs = []
    prev = None
    start = 0
    for qp in part_sizes(rows // col_count):
        part = qp * col_count
        piece = lt[:, :, start:start + part]
        start += part
        piece = jnp.swapaxes(piece, 0, 1).reshape(piece.shape[1], 2 * part)
        if prev is not None:
            piece = lax.optimization_barrier((piece, prev))[0]
        lall = lax.all_gather(piece, COL, axis=0, tiled=True)
        prev = lall
        q = dot(lall, rall)
        re = q[:part, :cols] - q[part:, cols:]
        im = q[:part, cols:] + q[part:, :cols]
        if start == rows:
            tile = jnp.stack([re.reshape(col_count, qp, cols), im.reshape(col_count, qp, cols)], axis=1)
            outs.append(scatter_cols(tile, col_count).reshape(2, 1, qp, col_count * cols))
        else:
            tile = jnp.stack([re, im], axis=0)
            tile = tile.reshape(2, col_count, qp, cols)
            outs.append(lax.all_to_all(tile, COL, split_axis=1, concat_axis=3, tiled=True))
    out = jnp.concatenate(outs, axis=2)
    return out.reshape(2, rows // col_count, col_count * cols)


def solution(mesh):
    devices = np.asarray(mesh.devices)
    nr, nc = devices.shape
    fine = Mesh(devices.reshape(2, nr // 2, 2, nc // 4, 2), ("xh", "z", "xl", "y", "core"))
    in_specs = (P(None, ROW, COL), P(None, ROW, COL), P(), P())
    out_specs = P(None, ROW + COL, None)
    return jax.shard_map(body, mesh=fine, in_specs=in_specs, out_specs=out_specs, check_vma=False)
```

```python
import functools

import jax
import jax.numpy as jnp
import numpy as np
from jax import lax
from jax.experimental import pallas as pl
from jax.experimental.pallas import tpu as pltpu
from jax.sharding import Mesh
from jax.sharding import PartitionSpec as P

LOW_BITS = 7
PREFIXES = 64

ROW = ("xh", "z")
CHIPS = ("xl", "y")
CORE = "core"
COL = ("xl", "y", "core")


def inverse_owner(prefix_owner, prefixes):
    labels = jnp.arange(prefixes, dtype=jnp.int32)
    match = (prefix_owner[None, :] == labels[:, None]).astype(jnp.int32)
    return jnp.sum(match * labels[None, :], axis=1)


def inner_order(qubit_order, low_bits):
    span = 2**low_bits
    offset = jnp.arange(span, dtype=jnp.int32)
    bits = jnp.bitwise_and(jnp.right_shift(offset[:, None], qubit_order[None, :]), 1)
    powers = jnp.left_shift(jnp.ones((low_bits,), jnp.int32), jnp.arange(low_bits, dtype=jnp.int32))
    return jnp.sum(bits * powers[None, :], axis=1)


def permute_left(left, prefix_owner, qubit_order, row_count, col_count):
    _, rows, kcols = left.shape
    span = 2**LOW_BITS
    local = rows // span
    sub = span // row_count
    x = left.reshape(2, local, row_count, sub, kcols)
    x = lax.all_to_all(x, ROW, split_axis=2, concat_axis=2, tiled=True)
    x = x.reshape(2, local * row_count, sub, kcols)
    inv = inverse_owner(prefix_owner, PREFIXES)
    pick = (inv % local) * row_count + inv // local
    y = jnp.take(x, pick, axis=1)
    y = y.reshape(2, row_count, local, sub, kcols)
    y = lax.all_to_all(y, ROW, split_axis=1, concat_axis=1, tiled=True)
    y = y.reshape(2, row_count * local * sub, kcols)
    s = inner_order(qubit_order, LOW_BITS)
    o_local = jnp.arange(local, dtype=jnp.int32)
    idx = (s[None, :] // sub) * (local * sub) + o_local[:, None] * sub + s[None, :] % sub
    idx = idx.reshape(-1)
    return jnp.take(y, jnp.take(idx, part_order(rows, col_count)), axis=1)


def part_sizes(q_total):
    return [q_total * 3 // 4, q_total - q_total * 3 // 4]


def part_order(rows, col_count):
    q_total = rows // col_count
    pos = []
    off = 0
    for qp in part_sizes(q_total):
        for c in range(col_count):
            pos.extend(c * q_total + off + i for i in range(qp))
        off += qp
    return np.asarray(pos, np.int32)


MESH_ID = pl.DeviceIdType.MESH


def scatter_kernel(ncol, tile_ref, out_ref, send, recv, own):
    xh, z = lax.axis_index("xh"), lax.axis_index("z")
    xl, y, core = lax.axis_index("xl"), lax.axis_index("y"), lax.axis_index("core")
    ys = ncol // 4
    me = (xl * ys + y) * 2 + core
    w = tile_ref.shape[-1]

    def col_dev(j):
        return (xh, z, j // (ys * 2), (j // 2) % ys, j % 2)

    barrier = pltpu.get_barrier_semaphore()
    for off in range(1, ncol):
        pl.semaphore_signal(barrier, 1, device_id=col_dev((me + off) % ncol), device_id_type=MESH_ID)
    pl.semaphore_wait(barrier, ncol - 1)

    dst = out_ref.at[:, :, pl.ds(pl.multiple_of(me * w, w), w)]
    local = pltpu.make_async_copy(tile_ref.at[me], dst, own.at[0])
    local.start()
    copies = []
    for off in range(1, ncol):
        j = (me + off) % ncol
        c = pltpu.make_async_remote_copy(
            tile_ref.at[j], dst, send.at[off], recv.at[off],
            device_id=col_dev(j), device_id_type=MESH_ID)
        c.start()
        copies.append(c)
    local.wait()
    for c in copies:
        c.wait()


def scatter_cols(tile, ncol):
    _, b, q, w = tile.shape
    return pl.pallas_call(
        functools.partial(scatter_kernel, ncol),
        out_shape=jax.ShapeDtypeStruct((b, q, ncol * w), tile.dtype),
        in_specs=[pl.BlockSpec(memory_space=pl.ANY)],
        out_specs=pl.BlockSpec(memory_space=pl.ANY),
        scratch_shapes=[
            pltpu.SemaphoreType.DMA((ncol,)),
            pltpu.SemaphoreType.DMA((ncol,)),
            pltpu.SemaphoreType.DMA((1,)),
        ],
        compiler_params=pltpu.CompilerParams(collective_id=0, has_side_effects=True),
    )(tile)


def body(left, right, prefix_owner, qubit_order):
    row_count = lax.axis_size(ROW)
    col_count = lax.axis_size(COL)
    rows = left.shape[1]
    cols = right.shape[2]
    rpiece = jnp.swapaxes(right, 0, 1).reshape(right.shape[1], 2 * cols)
    rall = lax.all_gather(rpiece, ROW, axis=0, tiled=True)
    lp = permute_left(left, prefix_owner, qubit_order, row_count, col_count)
    lt = jnp.swapaxes(lp, 1, 2)
    high = lax.Precision.HIGH
    dims = (((0,), (0,)), ((), ()))
    dot = lambda a, b: lax.dot_general(a, b, dims, preferred_element_type=jnp.float32, precision=high)
    outs = []
    prev = rall
    start = 0
    for qp in part_sizes(rows // col_count):
        part = qp * col_count
        piece = lt[:, :, start:start + part]
        start += part
        piece = jnp.swapaxes(piece, 0, 1).reshape(piece.shape[1], 2 * part)
        if prev is not None:
            piece = lax.optimization_barrier((piece, prev))[0]
        lall = lax.all_gather(piece, COL, axis=0, tiled=True)
        prev = lall
        q = dot(lall, rall)
        re = q[:part, :cols] - q[part:, cols:]
        im = q[:part, cols:] + q[part:, :cols]
        if start == rows:
            tile = jnp.stack([re.reshape(col_count, qp, cols), im.reshape(col_count, qp, cols)], axis=1)
            outs.append(scatter_cols(tile, col_count).reshape(2, 1, qp, col_count * cols))
        else:
            tile = jnp.stack([re, im], axis=0)
            tile = tile.reshape(2, col_count, qp, cols)
            outs.append(lax.all_to_all(tile, COL, split_axis=1, concat_axis=3, tiled=True))
    out = jnp.concatenate(outs, axis=2)
    return out.reshape(2, rows // col_count, col_count * cols)


def solution(mesh):
    devices = np.asarray(mesh.devices)
    nr, nc = devices.shape
    fine = Mesh(devices.reshape(2, nr // 2, 2, nc // 4, 2), ("xh", "z", "xl", "y", "core"))
    in_specs = (P(None, ROW, COL), P(None, ROW, COL), P(), P())
    out_specs = P(None, ROW + COL, None)
    return jax.shard_map(body, mesh=fine, in_specs=in_specs, out_specs=out_specs, check_vma=False)
```
